512 devices in a mesh: slab: 128 (over y, z, core), disk: 4 (over x).
Axes of the slice: x: 4, y: 8, z: 8, core: 2. Of those that a mesh axis runs over, the one named last changes fastest.
Arguments:
- thermal_anomaly: float32 [2, 128, 16384], P(None, 'slab', 'disk'), may hold values from 0.5 to 1.5
- humidity_amount: float32 [2, 128, 16384], P(None, 'slab', 'disk'), may hold values from 0.2 to 2
- slab_condensate_amount: float32 [2, 128, 16384], P(None, 'slab', 'disk'), may hold values from 0.1 to 2
- overcast_indicator: int32 [2, 16384], P(None, 'disk'), may hold values 0 or 1
- molecular_opacity: float32 [112, 128], replicated, may hold values from 0.003 to 0.1
- condensate_opacity: float32 [112], replicated, may hold values from 0.01 to 0.1
- planck_quadrature_factor: float32 [112], replicated, may hold values from 0.5 to 2
- scene_contributing_profiles: int32 [4, 262144], P(None, ('slab', 'disk')), may hold values from 0 to 16383, as said below
- scene_interpolation_factors: float32 [4, 262144], P(None, ('slab', 'disk')), may hold values from 0.1 to 1
Outputs:
- pixel_radiance: float32 [2, 16, 262144], P(None, None, ('slab', 'disk'))
The draws below stay inside these ranges and needn't reach their ends.
Inputs may be any that keep to these rules, and one draw needn't show every extreme that they name: `scene_contributing_profiles`: every source column c of pixel p lies in the pixel's latitude strip: (c % 4096) // 32 == p // 2048.
All inputs are finite; a program needn't handle non-finite values. No bound on the sum of `overcast_indicator` on one device may be relied on, other than what follows from the above.
Results may differ from the reference program's by a relative error of at most 0.0017.
Values may be sent and summed in bfloat16 or wider, within the bound.
No kernel may reach another device: no remote copies, remote signals or barrier semaphores. Data moves between devices by JAX's collectives and lax.ppermute only.
A program may use at most 64 MiB of HBM per device.

```python
import math
import jax
import jax.numpy as jnp
from jax import lax

COLS_DEV = 32
RESULT_TIMES = 2
G = 112
BANDS = 16
TAPS = 4
GPB = 7
VERTICAL_STEPS = 128
STRIP = 4096
GRID_PROFILES = 16384
PIX_ROW = 2048
PIXELS = 262144
N_DISK = 4


def draw_scene_contributing_profiles(key, part):
    key_owner, key_within = jax.random.split(key, 2)
    strip_row = jnp.arange(PIXELS) // PIX_ROW
    sector = jax.random.randint(key_owner, (TAPS, PIXELS), 0, N_DISK)
    within = jax.random.randint(key_within, (TAPS, PIXELS), 0, COLS_DEV)
    return (sector * STRIP + strip_row[None, :] * COLS_DEV + within).astype(jnp.int32)


def plant(entries, stream_key, smallest, top_value):
    spot = [jax.random.randint(jax.random.fold_in(stream_key, axis), (), 0, length) for axis, length in enumerate(entries.shape)]
    longest = entries.shape.index(max(entries.shape))
    neighbour = spot[:longest] + [(spot[longest] + 1) % entries.shape[longest]] + spot[longest + 1:]
    return entries.at[tuple(spot)].set(smallest).at[tuple(neighbour)].set(top_value)


def steps_of(stream_key, dims, cuts, smallest, top_value):
    level = 1.0
    for position, blocks in cuts:
        heights = jax.random.uniform(jax.random.fold_in(jax.random.fold_in(stream_key, 6), position), (blocks,), jnp.float32, smallest / len(cuts), top_value / len(cuts))
        level = level * jnp.repeat(jnp.exp(heights), dims[position] // blocks).reshape((-1,) + (1,) * (len(dims) - 1 - position))
    return level


def setup_inputs(seed: int = 0) -> dict:
    key_list = jax.random.split(jax.random.key(seed), 10)
    thermal_anomaly = jnp.clip(0.5 + 1.0 * jax.random.uniform(key_list[0], (RESULT_TIMES, VERTICAL_STEPS, GRID_PROFILES), jnp.float32) ** steps_of(key_list[0], (RESULT_TIMES, VERTICAL_STEPS, GRID_PROFILES), ((1, 128), (2, 4)), -0.2, 0.2), 0.5, 1.5)
    humidity_amount = jnp.clip(jnp.exp(math.log(2.0) - 2.3025851 * jax.random.uniform(key_list[1], (RESULT_TIMES, VERTICAL_STEPS, GRID_PROFILES), jnp.float32) ** steps_of(key_list[1], (RESULT_TIMES, VERTICAL_STEPS, GRID_PROFILES), ((1, 128), (2, 4)), -0.2, 0.2)), 0.2, 2.0)
    slab_condensate_amount = jnp.clip(jnp.exp(math.log(2.0) - 2.9957323 * jax.random.uniform(key_list[2], (RESULT_TIMES, VERTICAL_STEPS, GRID_PROFILES), jnp.float32) ** steps_of(key_list[2], (RESULT_TIMES, VERTICAL_STEPS, GRID_PROFILES), ((1, 128), (2, 4)), -0.2, 0.2)), 0.1, 2.0)
    overcast_indicator = plant((jax.random.randint(key_list[3], (RESULT_TIMES, GRID_PROFILES), 0, 2) < 1).astype(jnp.int32), jax.random.fold_in(key_list[3], 1), 0, 1)
    molecular_opacity = jnp.clip(jnp.exp(jax.random.uniform(key_list[4], (G, VERTICAL_STEPS), jnp.float32, math.log(0.003), math.log(0.1))), 0.003, 0.1)
    condensate_opacity = jnp.clip(jnp.exp(jax.random.uniform(key_list[5], (G,), jnp.float32, math.log(0.01), math.log(0.1))), 0.01, 0.1)
    planck_quadrature_factor = jnp.clip(jnp.exp(jax.random.uniform(key_list[6], (G,), jnp.float32, math.log(0.5), math.log(2.0))), 0.5, 2.0)
    scene_contributing_profiles = draw_scene_contributing_profiles(jax.random.fold_in(key_list[9], 71), 0)
    scene_interpolation_factors = jnp.clip(0.1 + 0.9 * jax.random.uniform(key_list[8], (TAPS, PIXELS), jnp.float32) ** steps_of(key_list[8], (TAPS, PIXELS), ((1, 512),), -0.2, 0.2), 0.1, 1.0)
    return {"thermal_anomaly": thermal_anomaly, "humidity_amount": humidity_amount, "slab_condensate_amount": slab_condensate_amount, "overcast_indicator": overcast_indicator, "molecular_opacity": molecular_opacity, "condensate_opacity": condensate_opacity, "planck_quadrature_factor": planck_quadrature_factor, "scene_contributing_profiles": scene_contributing_profiles, "scene_interpolation_factors": scene_interpolation_factors}


def band_block(temp_four, vapour_cols, cloud_cols, gas_band, cloud_band, planck_band):
    optical_depth = gas_band[:, :, None] * vapour_cols[None] + cloud_band[:, None, None] * cloud_cols[None]
    optical_depth_above = jnp.cumsum(optical_depth, axis=1) - optical_depth
    planck = planck_band[:, None, None] * temp_four[None]
    visible = jnp.exp(-optical_depth_above)
    emitted = jnp.sum(planck * visible * (1.0 - jnp.exp(-optical_depth)), axis=1)
    ground = planck[:, -1] * visible[:, -1] * jnp.exp(-optical_depth[:, -1])
    return jnp.sum(emitted + ground, axis=0) / gas_band.shape[0]


def radiate(temp_cols, vapour_cols, cloud_cols, molecular_opacity, condensate_opacity, planck_quadrature_factor):
    temp_four = temp_cols ** 4
    gas_bands = molecular_opacity.reshape(BANDS, GPB, VERTICAL_STEPS)
    cloud_bands = condensate_opacity.reshape(BANDS, GPB)
    planck_bands = planck_quadrature_factor.reshape(BANDS, GPB)

    def one_band(pieces):
        return band_block(temp_four, vapour_cols, cloud_cols, pieces[0], pieces[1], pieces[2])

    return lax.map(one_band, (gas_bands, cloud_bands, planck_bands))


def reference(thermal_anomaly, humidity_amount, slab_condensate_amount, overcast_indicator, molecular_opacity, condensate_opacity, planck_quadrature_factor, scene_contributing_profiles, scene_interpolation_factors):
    overcast_fraction_intensity = slab_condensate_amount * overcast_indicator.astype(jnp.float32)[:, None, :]
    blocks = GRID_PROFILES // COLS_DEV
    results = []
    for hour in range(RESULT_TIMES):
        def collect_profiles_again(field):
            return field[hour].reshape(VERTICAL_STEPS, blocks, COLS_DEV).transpose(1, 0, 2)

        def lone_partition(pieces):
            return radiate(pieces[0], pieces[1], pieces[2], molecular_opacity, condensate_opacity, planck_quadrature_factor)

        spectral_interval_intensity = lax.map(lone_partition, (collect_profiles_again(thermal_anomaly), collect_profiles_again(humidity_amount), collect_profiles_again(overcast_fraction_intensity)))
        spectral_interval_intensity = spectral_interval_intensity.transpose(1, 0, 2).reshape(BANDS, GRID_PROFILES).astype(jnp.bfloat16)
        picked = spectral_interval_intensity[:, scene_contributing_profiles].astype(jnp.float32)
        results.append(jnp.sum(picked * scene_interpolation_factors[None], axis=1))
    return jnp.stack(results)
```

```python
import jax
import jax.numpy as jnp
from jax import lax
from jax.experimental import pallas as pl
from jax.experimental.pallas import tpu as pltpu
from jax.sharding import PartitionSpec as P

HOURS = 2
BANDS = 16
GPB = 7
LEVELS = 128
TAPS = 4
COLS = 32
DISKS = 4
SECTOR = 4096
PIX = 512
HALF = BANDS // 2
LANES = 128
LOG2E = 1.4426950408889634

HUM_LOW, HUM_STEP = 0.2, 1.8 / 65535.0
CON_LOW, CON_STEP = 0.1, 1.9 / 65535.0
T4_SCALE = float(2**28)


def code16(x, low, step):
    q = ((x - low) * (1.0 / step) + 0.5).astype(jnp.int32)
    return jnp.clip(q, 0, 65535)


def pack_kernel(temp_ref, hum_ref, con_ref, out_ref):
    rows = SECTOR // LANES
    t2 = temp_ref[...] * temp_ref[...]
    t4 = (t2 * t2 * T4_SCALE).astype(jnp.int32)
    hum = code16(hum_ref[...], HUM_LOW, HUM_STEP)
    con = code16(con_ref[...], CON_LOW, CON_STEP)
    gas = (hum << 16) | con
    parts = (gas[:rows], gas[rows:], t4[:rows], t4[rows:])
    lane = lax.broadcasted_iota(jnp.int32, (rows, LANES), 1) // COLS
    for dest in range(LANES // COLS):
        word = None
        for spot, part in enumerate(parts):
            shift = (spot - dest) % 4 * COLS
            moved = pltpu.roll(part, shift, 1) if shift else part
            word = moved if word is None else jnp.where(lane == spot, moved, word)
        out_ref[pl.ds(dest, rows, stride=LANES // COLS), :] = word


def spread_kernel(mol_ref, con_ref, planck_ref, gas_ref, cloud_ref, weight_ref):
    lane = lax.broadcasted_iota(jnp.int32, (HALF, LANES), 1)
    row = lax.broadcasted_iota(jnp.int32, (HALF, LANES), 0)
    first = lane < LANES // 2
    con = jnp.broadcast_to(con_ref[...], (HALF, con_ref.shape[1]))
    planck = jnp.broadcast_to(planck_ref[...], (HALF, planck_ref.shape[1]))
    glane = lax.broadcasted_iota(jnp.int32, con.shape, 1)
    grow = lax.broadcasted_iota(jnp.int32, con.shape, 0)

    def column(values, j):
        low = jnp.sum(jnp.where(glane == grow * GPB + j, values, 0.0), axis=1, keepdims=True)
        high = jnp.sum(
            jnp.where(glane == (grow + HALF) * GPB + j, values, 0.0), axis=1, keepdims=True
        )
        return jnp.where(
            first, jnp.broadcast_to(low, (HALF, LANES)), jnp.broadcast_to(high, (HALF, LANES))
        )

    for j in range(GPB):
        cloud_ref[j] = column(con, j) * -LOG2E
        weight_ref[j] = column(planck, j)

    def block(i, _):
        for j in range(GPB):
            low = mol_ref[pl.ds(j, HALF, stride=GPB), :] * -LOG2E
            high = mol_ref[pl.ds(HALF * GPB + j, HALF, stride=GPB), :] * -LOG2E
            low = pltpu.roll(low, LANES - 8 * i, 1)
            high = pltpu.roll(high, LANES - 8 * i, 1)
            for k in range(8):
                gas_ref[8 * i + k, j] = jnp.where(
                    first,
                    jnp.broadcast_to(low[:, k : k + 1], (HALF, LANES)),
                    jnp.broadcast_to(high[:, k : k + 1], (HALF, LANES)),
                )
        return 0

    lax.fori_loop(0, LEVELS // 8, block, 0)


def radiate_kernel(
    word_ref, over_ref, gas_ref, cloud_ref, weight_ref, out_ref, hum_ref, con_ref, t4_ref, diff_ref
):
    strip = lax.axis_index("slab")
    group = LANES // COLS
    block = over_ref[:, pl.ds(pl.multiple_of(strip // group * LANES, LANES), LANES)]
    lane8 = lax.broadcasted_iota(jnp.int32, (8, LANES), 1) // COLS
    overcast = None
    for spot in range(group):
        hour = spot % HOURS
        row = jnp.broadcast_to(block[hour : hour + 1], (8, LANES))
        row = pltpu.roll(row, (spot - strip % group + group) % group * COLS, 1)
        overcast = row if overcast is None else jnp.where(lane8 == spot, row, overcast)
    overcast = overcast[0:1].astype(jnp.float32)

    word = word_ref[...]
    swapped = pltpu.roll(word, LANES // 2, 1)
    first = lax.broadcasted_iota(jnp.int32, word.shape, 1) < LANES // 2
    gas = jnp.where(first, word, swapped)
    t4 = jnp.where(first, swapped, word)
    hum = lax.shift_right_logical(gas, 16)
    con = gas & 65535
    hum_ref[...] = hum.astype(jnp.float32) * HUM_STEP + HUM_LOW
    con_ref[...] = (con.astype(jnp.float32) * CON_STEP + CON_LOW) * overcast
    t4_ref[pl.ds(0, LEVELS), :] = t4.astype(jnp.float32) * (1.0 / T4_SCALE)
    t4_ref[pl.ds(LEVELS, 1), :] = t4_ref[pl.ds(LEVELS - 1, 1), :]
    diff_ref[...] = t4_ref[pl.ds(1, LEVELS), :] - t4_ref[pl.ds(0, LEVELS), :]

    zero = jnp.zeros((HALF, LANES), jnp.float32)
    clouds = [cloud_ref[j] for j in range(GPB)]

    def step(i, carry):
        depth, total = list(carry[0]), list(carry[1])
        for k in range(8):
            level = 8 * i + k
            hum_row = hum_ref[pl.ds(level, HALF, stride=0), :]
            con_row = con_ref[pl.ds(level, HALF, stride=0), :]
            diff_row = diff_ref[pl.ds(level, HALF, stride=0), :]
            for j in range(GPB):
                depth[j] = depth[j] + (gas_ref[level, j] * hum_row + clouds[j] * con_row)
                total[j] = total[j] + diff_row * jnp.exp2(depth[j])
        return tuple(depth), tuple(total)

    _, total = lax.fori_loop(0, LEVELS // 8, step, ((zero,) * GPB, (zero,) * GPB))
    top = t4_ref[pl.ds(0, HALF, stride=0), :]
    band = zero
    for j in range(GPB):
        band = band + weight_ref[j] * (top + total[j])
    band = (band / GPB).astype(jnp.bfloat16).astype(jnp.float32)
    for owner in range(DISKS):
        out_ref[owner] = band


def pixel_kernel(rad_ref, source_ref, factor_ref, out_ref):
    lane = lax.broadcasted_iota(jnp.int32, (HALF, LANES), 1) // COLS
    rows = []
    for hour in range(HOURS):
        for half in range(2):
            spot = half * HOURS + hour
            row = None
            for disk in range(DISKS):
                shift = (disk - spot) % 4 * COLS
                moved = rad_ref[disk]
                moved = pltpu.roll(moved, shift, 1) if shift else moved
                row = moved if row is None else jnp.where(lane == disk, moved, row)
            rows.append(row)
    rad = jnp.concatenate(rows, axis=0).astype(jnp.bfloat16)
    strip_cols = DISKS * COLS
    col = lax.broadcasted_iota(jnp.int32, (strip_cols, PIX), 0)
    source = source_ref[...]
    local = source // SECTOR * COLS + source % COLS
    mix = jnp.zeros((strip_cols, PIX), jnp.float32)
    for tap in range(TAPS):
        mix = mix + jnp.where(col == local[tap : tap + 1], factor_ref[tap : tap + 1, :], 0.0)
    high = mix.astype(jnp.bfloat16)
    low = (mix - high.astype(jnp.float32)).astype(jnp.bfloat16)
    out_ref[...] = jnp.dot(rad, high, preferred_element_type=jnp.float32) + jnp.dot(
        rad, low, preferred_element_type=jnp.float32
    )


def local(
    thermal_anomaly,
    humidity_amount,
    slab_condensate_amount,
    overcast_indicator,
    molecular_opacity,
    condensate_opacity,
    planck_quadrature_factor,
    scene_contributing_profiles,
    scene_interpolation_factors,
):
    f32 = jnp.float32
    rows = HOURS * SECTOR // LANES
    with jax.named_scope("pack"):
        words = pl.pallas_call(
            pack_kernel, out_shape=jax.ShapeDtypeStruct((LEVELS, LANES), jnp.int32)
        )(
            thermal_anomaly.reshape(rows, LANES),
            humidity_amount.reshape(rows, LANES),
            slab_condensate_amount.reshape(rows, LANES),
        )
    words = lax.all_to_all(words, "slab", split_axis=0, concat_axis=0, tiled=True)
    with jax.named_scope("spread"):
        gas, cloud, weight = pl.pallas_call(
            spread_kernel,
            out_shape=(
                jax.ShapeDtypeStruct((LEVELS, GPB, HALF, LANES), f32),
                jax.ShapeDtypeStruct((GPB, HALF, LANES), f32),
                jax.ShapeDtypeStruct((GPB, HALF, LANES), f32),
            ),
        )(
            molecular_opacity,
            condensate_opacity.reshape(1, -1),
            planck_quadrature_factor.reshape(1, -1),
        )
    with jax.named_scope("radiate"):
        level_cols = pltpu.VMEM((LEVELS, LANES), f32)
        radiance = pl.pallas_call(
            radiate_kernel,
            out_shape=jax.ShapeDtypeStruct((DISKS, HALF, LANES), f32),
            scratch_shapes=[level_cols, level_cols, pltpu.VMEM((LEVELS + 8, LANES), f32), level_cols],
        )(words, overcast_indicator, gas, cloud, weight)
    radiance = lax.all_to_all(radiance, "disk", split_axis=0, concat_axis=0, tiled=True)
    with jax.named_scope("pixels"):
        pixels = pl.pallas_call(
            pixel_kernel, out_shape=jax.ShapeDtypeStruct((HOURS * BANDS, PIX), f32)
        )(radiance, scene_contributing_profiles, scene_interpolation_factors)
    return pixels.reshape(HOURS, BANDS, PIX)


def solution(mesh):
    in_specs = (
        P(None, "slab", "disk"),
        P(None, "slab", "disk"),
        P(None, "slab", "disk"),
        P(None, "disk"),
        P(),
        P(),
        P(),
        P(None, ("slab", "disk")),
        P(None, ("slab", "disk")),
    )
    out_specs = P(None, None, ("slab", "disk"))
    return jax.shard_map(local, mesh=mesh, in_specs=in_specs, out_specs=out_specs, check_vma=False)
```

```python
import jax
import jax.numpy as jnp
from jax import lax
from jax.experimental import pallas as pl
from jax.experimental.pallas import tpu as pltpu
from jax.sharding import PartitionSpec as P

HOURS = 2
BANDS = 16
GPB = 7
LEVELS = 128
TAPS = 4
COLS = 32
DISKS = 4
SECTOR = 4096
PIX = 512
HALF = BANDS // 2
LANES = 128
KEPT = 96
LOG2E = 1.4426950408889634

HUM_LOW, HUM_STEP = 0.2, 1.8 / 65535.0
CON_LOW, CON_STEP = 0.1, 1.9 / 65535.0
T4_SCALE = float(2**28)


def code16(x, low, step):
    q = ((x - low) * (1.0 / step) + 0.5).astype(jnp.int32)
    return jnp.clip(q, 0, 65535)


def pack_kernel(temp_ref, hum_ref, con_ref, out_ref):
    rows = SECTOR // LANES
    t2 = temp_ref[...] * temp_ref[...]
    t4 = (t2 * t2 * T4_SCALE).astype(jnp.int32)
    hum = code16(hum_ref[...], HUM_LOW, HUM_STEP)
    con = code16(con_ref[...], CON_LOW, CON_STEP)
    gas = (hum << 16) | con
    parts = (gas[:rows], gas[rows:], t4[:rows], t4[rows:])
    lane = lax.broadcasted_iota(jnp.int32, (rows, LANES), 1) // COLS
    for dest in range(LANES // COLS):
        word = None
        for spot, part in enumerate(parts):
            moved = turn(part, (spot - dest) % 4 * COLS)
            word = moved if word is None else jnp.where(lane == spot, moved, word)
        out_ref[pl.ds(dest, rows, stride=LANES // COLS), :] = word


def turn(x, shift):
    return x if isinstance(shift, int) and shift == 0 else pltpu.roll(x, shift, 1)


def prepare_kernel(
    mol_ref, con_ref, planck_ref, over_ref, source_ref, factor_ref,
    gas_ref, low_gas_ref, cloud_ref, weight_ref, overcast_ref, mix_ref,
):
    lane = lax.broadcasted_iota(jnp.int32, (HALF, LANES), 1)
    first = lane < LANES // 2
    con = jnp.broadcast_to(con_ref[...], (HALF, con_ref.shape[1]))
    planck = jnp.broadcast_to(planck_ref[...], (HALF, planck_ref.shape[1]))
    glane = lax.broadcasted_iota(jnp.int32, con.shape, 1)
    grow = lax.broadcasted_iota(jnp.int32, con.shape, 0)

    def column(values, j):
        low = jnp.sum(jnp.where(glane == grow * GPB + j, values, 0.0), axis=1, keepdims=True)
        high = jnp.sum(
            jnp.where(glane == (grow + HALF) * GPB + j, values, 0.0), axis=1, keepdims=True
        )
        return jnp.where(
            first, jnp.broadcast_to(low, (HALF, LANES)), jnp.broadcast_to(high, (HALF, LANES))
        )

    for j in range(GPB):
        cloud_ref[j] = column(con, j) * -LOG2E
        weight_ref[j] = column(planck, j)

    span = LANES // 4
    shape = (span * HALF, LANES)
    pick = lax.broadcasted_iota(jnp.int32, shape, 1) % span == (
        lax.broadcasted_iota(jnp.int32, shape, 0) // HALF
    )
    half_of = lambda axis: lax.broadcasted_iota(jnp.int32, (LANES, LANES), axis) // (LANES // 2)
    same_half = (half_of(0) == half_of(1)).astype(jnp.float32).astype(jnp.bfloat16)

    def levels(q, first_level, to_ref):
        for j in range(GPB):
            row = None
            for half in range(2):
                tile = mol_ref[pl.ds(half * HALF * GPB + j, HALF, stride=GPB), :] * -LOG2E
                high = tile.astype(jnp.bfloat16).astype(jnp.float32)
                for k, piece in enumerate((high, tile - high)):
                    spot = 2 * half + k
                    moved = turn(piece, (spot - q + 4) % 4 * span)
                    row = moved if row is None else jnp.where(lane // span == spot, moved, row)
            rows = jnp.broadcast_to(row[None], (span, HALF, LANES)).reshape(shape)
            rows = jnp.where(pick, rows, 0.0).astype(jnp.bfloat16)
            wide = jnp.dot(rows, same_half, preferred_element_type=jnp.float32)
            start = pl.multiple_of(first_level, span)
            to_ref[pl.ds(start, span), j] = wide.reshape(span, HALF, LANES)
        return 0

    levels(KEPT // span, 0, low_gas_ref)
    lax.fori_loop(0, KEPT // span, lambda q, _: levels(q, q * span, gas_ref), 0)

    strip = lax.axis_index("slab")
    group = LANES // COLS
    block = over_ref[:, pl.ds(pl.multiple_of(strip // group * LANES, LANES), LANES)]
    overcast = None
    for spot in range(group):
        row = jnp.broadcast_to(block[spot % HOURS : spot % HOURS + 1], (HALF, LANES))
        row = pltpu.roll(row, (spot - strip % group + group) % group * COLS, 1)
        overcast = row if overcast is None else jnp.where(lane // COLS == spot, row, overcast)
    overcast_ref[...] = overcast.astype(jnp.float32)

    strip_cols = DISKS * COLS
    col = lax.broadcasted_iota(jnp.int32, (strip_cols, PIX), 0)
    source = source_ref[...]
    local = source // SECTOR * COLS + source % COLS
    mix = jnp.zeros((strip_cols, PIX), jnp.float32)
    for tap in range(TAPS):
        mix = mix + jnp.where(col == local[tap : tap + 1], factor_ref[tap : tap + 1, :], 0.0)
    high = mix.astype(jnp.bfloat16)
    mix_ref[pl.ds(0, strip_cols), :] = high
    mix_ref[pl.ds(strip_cols, strip_cols), :] = (mix - high.astype(jnp.float32)).astype(jnp.bfloat16)


def radiate_kernel(
    word_ref, gas_ref, low_gas_ref, cloud_ref, weight_ref, overcast_ref,
    out_ref,
    tail_ref, hum_ref, con_ref, t4_ref, diff_ref, sem,
):
    copy = pltpu.make_async_copy(low_gas_ref, tail_ref, sem)
    copy.start()
    word = word_ref[...]
    swapped = pltpu.roll(word, LANES // 2, 1)
    first = lax.broadcasted_iota(jnp.int32, word.shape, 1) < LANES // 2
    gas = jnp.where(first, word, swapped)
    t4 = jnp.where(first, swapped, word)
    hum = lax.shift_right_logical(gas, 16)
    con = gas & 65535
    hum_ref[...] = hum.astype(jnp.float32) * HUM_STEP + HUM_LOW
    con_ref[...] = (con.astype(jnp.float32) * CON_STEP + CON_LOW) * overcast_ref[0:1, :]
    t4_ref[pl.ds(0, LEVELS), :] = t4.astype(jnp.float32) * (1.0 / T4_SCALE)
    t4_ref[pl.ds(LEVELS, 1), :] = t4_ref[pl.ds(LEVELS - 1, 1), :]
    diff_ref[...] = t4_ref[pl.ds(1, LEVELS), :] - t4_ref[pl.ds(0, LEVELS), :]

    zero = jnp.zeros((HALF, LANES), jnp.float32)
    clouds = [cloud_ref[j] for j in range(GPB)]

    def step(i, carry, from_ref, start):
        depth, total = list(carry[0]), list(carry[1])
        for k in range(8):
            level = 8 * i + k
            hum_row = hum_ref[pl.ds(start + level, HALF, stride=0), :]
            con_row = con_ref[pl.ds(start + level, HALF, stride=0), :]
            diff_row = diff_ref[pl.ds(start + level, HALF, stride=0), :]
            for j in range(GPB):
                depth[j] = depth[j] + (from_ref[level, j] * hum_row + clouds[j] * con_row)
                total[j] = total[j] + diff_row * jnp.exp2(depth[j])
        return tuple(depth), tuple(total)

    carry = (zero,) * GPB, (zero,) * GPB
    carry = lax.fori_loop(0, KEPT // 8, lambda i, c: step(i, c, gas_ref, 0), carry)
    copy.wait()
    _, total = lax.fori_loop(
        0, (LEVELS - KEPT) // 8, lambda i, c: step(i, c, tail_ref, KEPT), carry
    )
    top = t4_ref[pl.ds(0, HALF, stride=0), :]
    band = zero
    for j in range(GPB):
        band = band + weight_ref[j] * (top + total[j])
    band = (band / GPB).astype(jnp.bfloat16).astype(jnp.float32)
    for owner in range(DISKS):
        out_ref[owner] = band


def pixel_kernel(rad_ref, mix_ref, out_ref):
    lane = lax.broadcasted_iota(jnp.int32, (HALF, LANES), 1) // COLS
    rows = []
    for hour in range(HOURS):
        for half in range(2):
            spot = half * HOURS + hour
            row = None
            for disk in range(DISKS):
                moved = turn(rad_ref[disk], (disk - spot) % 4 * COLS)
                row = moved if row is None else jnp.where(lane == disk, moved, row)
            rows.append(row)
    rad = jnp.concatenate(rows, axis=0).astype(jnp.bfloat16)
    rad = jnp.concatenate([rad, rad], axis=1)
    out_ref[...] = jnp.dot(rad, mix_ref[...], preferred_element_type=jnp.float32)


ANY = pl.BlockSpec(memory_space=pl.ANY)
SMALL = pltpu.CompilerParams(vmem_limit_bytes=8 << 20)


def in_vmem(x):
    return pltpu.with_memory_space_constraint(x, pltpu.VMEM)


def in_hbm(x):
    return pltpu.with_memory_space_constraint(x, pltpu.HBM)


def local(
    thermal_anomaly,
    humidity_amount,
    slab_condensate_amount,
    overcast_indicator,
    molecular_opacity,
    condensate_opacity,
    planck_quadrature_factor,
    scene_contributing_profiles,
    scene_interpolation_factors,
):
    f32 = jnp.float32
    rows = HOURS * SECTOR // LANES
    level_cols = pltpu.VMEM((LEVELS, LANES), f32)
    per_point = pltpu.VMEM((GPB, HALF, LANES), f32)
    with jax.named_scope("pack"):
        words = pl.pallas_call(
            pack_kernel, out_shape=pltpu.VMEM((LEVELS, LANES), jnp.int32), compiler_params=SMALL
        )(
            in_hbm(thermal_anomaly.reshape(rows, LANES)),
            in_hbm(humidity_amount.reshape(rows, LANES)),
            in_hbm(slab_condensate_amount.reshape(rows, LANES)),
        )
    words = lax.all_to_all(words, "slab", split_axis=0, concat_axis=0, tiled=True)
    with jax.named_scope("prepare"):
        gas, low_gas, cloud, weight, overcast, mix = pl.pallas_call(
            prepare_kernel,
            out_shape=(
                pltpu.VMEM((KEPT, GPB, HALF, LANES), f32),
                pltpu.HBM((LEVELS - KEPT, GPB, HALF, LANES), f32),
                per_point,
                per_point,
                pltpu.VMEM((HALF, LANES), f32),
                pltpu.VMEM((2 * DISKS * COLS, PIX), jnp.bfloat16),
            ),
            compiler_params=SMALL,
        )(
            in_hbm(molecular_opacity),
            in_hbm(condensate_opacity.reshape(1, -1)),
            in_hbm(planck_quadrature_factor.reshape(1, -1)),
            in_hbm(overcast_indicator),
            in_hbm(scene_contributing_profiles),
            in_hbm(scene_interpolation_factors),
        )
    with jax.named_scope("radiate"):
        radiance = pl.pallas_call(
            radiate_kernel,
            out_shape=pltpu.VMEM((DISKS, HALF, LANES), f32),
            in_specs=[ANY if k == 2 else pl.BlockSpec() for k in range(6)],
            scratch_shapes=[
                pltpu.VMEM((LEVELS - KEPT, GPB, HALF, LANES), f32),
                level_cols,
                level_cols,
                pltpu.VMEM((LEVELS + 8, LANES), f32),
                level_cols,
                pltpu.SemaphoreType.DMA,
            ],
            compiler_params=SMALL,
        )(in_vmem(words), gas, in_hbm(low_gas), cloud, weight, overcast)
    radiance = lax.all_to_all(radiance, "disk", split_axis=0, concat_axis=0, tiled=True)
    with jax.named_scope("pixels"):
        pixels = pl.pallas_call(
            pixel_kernel,
            out_shape=jax.ShapeDtypeStruct((HOURS * BANDS, PIX), f32),
            compiler_params=SMALL,
        )(in_vmem(radiance), mix)
    return pixels.reshape(HOURS, BANDS, PIX)


def solution(mesh):
    in_specs = (
        P(None, "slab", "disk"),
        P(None, "slab", "disk"),
        P(None, "slab", "disk"),
        P(None, "disk"),
        P(),
        P(),
        P(),
        P(None, ("slab", "disk")),
        P(None, ("slab", "disk")),
    )
    out_specs = P(None, None, ("slab", "disk"))
    return jax.shard_map(local, mesh=mesh, in_specs=in_specs, out_specs=out_specs, check_vma=False)
```

```python
import jax
import jax.numpy as jnp
from jax import lax
from jax.experimental import pallas as pl
from jax.experimental.pallas import tpu as pltpu
from jax.sharding import PartitionSpec as P

HOURS = 2
BANDS = 16
GPB = 7
LEVELS = 128
TAPS = 4
COLS = 32
DISKS = 4
SECTOR = 4096
PIX = 512
HALF = BANDS // 2
LANES = 128
FIRST_SLAB = 108
FIRST_DISK = 2
KEPT = 96
LOG2E = 1.4426950408889634

HUM_LOW, HUM_STEP = 0.2, 1.8 / 65535.0
CON_LOW, CON_STEP = 0.1, 1.9 / 65535.0
T4_SCALE = float(2**28)


def code16(x, low, step):
    q = ((x - low) * (1.0 / step) + 0.5).astype(jnp.int32)
    return jnp.clip(q, 0, 65535)


def swapped_group(size, first):
    return [first if i == 0 else 0 if i == first else i for i in range(size)]


def swap_rows(ref):
    if FIRST_SLAB:
        held = ref[0:1, :]
        ref[0:1, :] = ref[FIRST_SLAB : FIRST_SLAB + 1, :]
        ref[FIRST_SLAB : FIRST_SLAB + 1, :] = held


def pack_kernel(temp_ref, hum_ref, con_ref, out_ref):
    rows = SECTOR // LANES
    t2 = temp_ref[...] * temp_ref[...]
    t4 = (t2 * t2 * T4_SCALE).astype(jnp.int32)
    hum = code16(hum_ref[...], HUM_LOW, HUM_STEP)
    con = code16(con_ref[...], CON_LOW, CON_STEP)
    gas = (hum << 16) | con
    parts = (gas[:rows], gas[rows:], t4[:rows], t4[rows:])
    lane = lax.broadcasted_iota(jnp.int32, (rows, LANES), 1) // COLS
    for dest in range(LANES // COLS):
        word = None
        for spot, part in enumerate(parts):
            moved = turn(part, (spot - dest) % 4 * COLS)
            word = moved if word is None else jnp.where(lane == spot, moved, word)
        out_ref[pl.ds(dest, rows, stride=LANES // COLS), :] = word
    swap_rows(out_ref)


def turn(x, shift):
    return x if isinstance(shift, int) and shift == 0 else pltpu.roll(x, shift, 1)


def prepare_kernel(
    mol_ref, con_ref, planck_ref, over_ref, source_ref, factor_ref,
    gas_ref, low_gas_ref, cloud_ref, weight_ref, overcast_ref, mix_ref,
):
    lane = lax.broadcasted_iota(jnp.int32, (HALF, LANES), 1)
    first = lane < LANES // 2
    con = jnp.broadcast_to(con_ref[...], (HALF, con_ref.shape[1]))
    planck = jnp.broadcast_to(planck_ref[...], (HALF, planck_ref.shape[1]))
    glane = lax.broadcasted_iota(jnp.int32, con.shape, 1)
    grow = lax.broadcasted_iota(jnp.int32, con.shape, 0)

    def column(values, j):
        low = jnp.sum(jnp.where(glane == grow * GPB + j, values, 0.0), axis=1, keepdims=True)
        high = jnp.sum(
            jnp.where(glane == (grow + HALF) * GPB + j, values, 0.0), axis=1, keepdims=True
        )
        return jnp.where(
            first, jnp.broadcast_to(low, (HALF, LANES)), jnp.broadcast_to(high, (HALF, LANES))
        )

    for j in range(GPB):
        cloud_ref[j] = column(con, j) * -LOG2E
        weight_ref[j] = column(planck, j)

    span = LANES // 4
    shape = (span * HALF, LANES)
    pick = lax.broadcasted_iota(jnp.int32, shape, 1) % span == (
        lax.broadcasted_iota(jnp.int32, shape, 0) // HALF
    )
    half_of = lambda axis: lax.broadcasted_iota(jnp.int32, (LANES, LANES), axis) // (LANES // 2)
    same_half = (half_of(0) == half_of(1)).astype(jnp.float32).astype(jnp.bfloat16)

    def levels(q, first_level, to_ref):
        for j in range(GPB):
            row = None
            for half in range(2):
                tile = mol_ref[pl.ds(half * HALF * GPB + j, HALF, stride=GPB), :] * -LOG2E
                high = tile.astype(jnp.bfloat16).astype(jnp.float32)
                for k, piece in enumerate((high, tile - high)):
                    spot = 2 * half + k
                    moved = turn(piece, (spot - q + 4) % 4 * span)
                    row = moved if row is None else jnp.where(lane // span == spot, moved, row)
            rows = jnp.broadcast_to(row[None], (span, HALF, LANES)).reshape(shape)
            rows = jnp.where(pick, rows, 0.0).astype(jnp.bfloat16)
            wide = jnp.dot(rows, same_half, preferred_element_type=jnp.float32)
            start = pl.multiple_of(first_level, span)
            to_ref[pl.ds(start, span), j] = wide.reshape(span, HALF, LANES)
        return 0

    levels(KEPT // span, 0, low_gas_ref)
    lax.fori_loop(0, KEPT // span, lambda q, _: levels(q, q * span, gas_ref), 0)

    strip = lax.axis_index("slab")
    group = LANES // COLS
    block = over_ref[:, pl.ds(pl.multiple_of(strip // group * LANES, LANES), LANES)]
    overcast = None
    for spot in range(group):
        row = jnp.broadcast_to(block[spot % HOURS : spot % HOURS + 1], (HALF, LANES))
        row = pltpu.roll(row, (spot - strip % group + group) % group * COLS, 1)
        overcast = row if overcast is None else jnp.where(lane // COLS == spot, row, overcast)
    overcast_ref[...] = overcast.astype(jnp.float32)

    strip_cols = DISKS * COLS
    col = lax.broadcasted_iota(jnp.int32, (strip_cols, PIX), 0)
    source = source_ref[...]
    local = source // SECTOR * COLS + source % COLS
    mix = jnp.zeros((strip_cols, PIX), jnp.float32)
    for tap in range(TAPS):
        mix = mix + jnp.where(col == local[tap : tap + 1], factor_ref[tap : tap + 1, :], 0.0)
    high = mix.astype(jnp.bfloat16)
    mix_ref[pl.ds(0, strip_cols), :] = high
    mix_ref[pl.ds(strip_cols, strip_cols), :] = (mix - high.astype(jnp.float32)).astype(jnp.bfloat16)


def radiate_kernel(
    word_ref, gas_ref, low_gas_ref, cloud_ref, weight_ref, overcast_ref,
    out_ref,
    tail_ref, hum_ref, con_ref, t4_ref, diff_ref, sem,
):
    copy = pltpu.make_async_copy(low_gas_ref, tail_ref, sem)
    copy.start()
    word = word_ref[...]
    swapped = pltpu.roll(word, LANES // 2, 1)
    first = lax.broadcasted_iota(jnp.int32, word.shape, 1) < LANES // 2
    gas = jnp.where(first, word, swapped)
    t4 = jnp.where(first, swapped, word)
    hum = lax.shift_right_logical(gas, 16)
    con = gas & 65535
    hum_ref[...] = hum.astype(jnp.float32) * HUM_STEP + HUM_LOW
    con_ref[...] = (con.astype(jnp.float32) * CON_STEP + CON_LOW) * overcast_ref[0:1, :]
    t4_ref[pl.ds(0, LEVELS), :] = t4.astype(jnp.float32) * (1.0 / T4_SCALE)
    for by_sender in (hum_ref, con_ref, t4_ref):
        swap_rows(by_sender)
    t4_ref[pl.ds(LEVELS, 1), :] = t4_ref[pl.ds(LEVELS - 1, 1), :]
    diff_ref[...] = t4_ref[pl.ds(1, LEVELS), :] - t4_ref[pl.ds(0, LEVELS), :]

    zero = jnp.zeros((HALF, LANES), jnp.float32)
    clouds = [cloud_ref[j] for j in range(GPB)]

    def step(i, carry, from_ref, start):
        depth, total = list(carry[0]), list(carry[1])
        for k in range(8):
            level = 8 * i + k
            hum_row = hum_ref[pl.ds(start + level, HALF, stride=0), :]
            con_row = con_ref[pl.ds(start + level, HALF, stride=0), :]
            diff_row = diff_ref[pl.ds(start + level, HALF, stride=0), :]
            for j in range(GPB):
                depth[j] = depth[j] + (from_ref[level, j] * hum_row + clouds[j] * con_row)
                total[j] = total[j] + diff_row * jnp.exp2(depth[j])
        return tuple(depth), tuple(total)

    carry = (zero,) * GPB, (zero,) * GPB
    carry = lax.fori_loop(0, KEPT // 8, lambda i, c: step(i, c, gas_ref, 0), carry)
    copy.wait()
    _, total = lax.fori_loop(
        0, (LEVELS - KEPT) // 8, lambda i, c: step(i, c, tail_ref, KEPT), carry
    )
    top = t4_ref[pl.ds(0, HALF, stride=0), :]
    band = zero
    for j in range(GPB):
        band = band + weight_ref[j] * (top + total[j])
    band = (band / GPB).astype(jnp.bfloat16).astype(jnp.float32)
    for owner in range(DISKS):
        out_ref[owner] = band


def pixel_kernel(rad_ref, mix_ref, out_ref):
    lane = lax.broadcasted_iota(jnp.int32, (HALF, LANES), 1) // COLS
    sender = swapped_group(DISKS, FIRST_DISK)
    rows = []
    for hour in range(HOURS):
        for half in range(2):
            spot = half * HOURS + hour
            row = None
            for disk in range(DISKS):
                moved = turn(rad_ref[sender.index(disk)], (disk - spot) % 4 * COLS)
                row = moved if row is None else jnp.where(lane == disk, moved, row)
            rows.append(row)
    rad = jnp.concatenate(rows, axis=0).astype(jnp.bfloat16)
    rad = jnp.concatenate([rad, rad], axis=1)
    out_ref[...] = jnp.dot(rad, mix_ref[...], preferred_element_type=jnp.float32)


ANY = pl.BlockSpec(memory_space=pl.ANY)
SMALL = pltpu.CompilerParams(vmem_limit_bytes=8 << 20)


def in_vmem(x):
    return pltpu.with_memory_space_constraint(x, pltpu.VMEM)


def in_hbm(x):
    return pltpu.with_memory_space_constraint(x, pltpu.HBM)


def exchange(x, axis, first):
    group = swapped_group(lax.axis_size(axis), first)
    return lax.all_to_all(x, axis, 0, 0, axis_index_groups=[group], tiled=True)


def local(
    thermal_anomaly,
    humidity_amount,
    slab_condensate_amount,
    overcast_indicator,
    molecular_opacity,
    condensate_opacity,
    planck_quadrature_factor,
    scene_contributing_profiles,
    scene_interpolation_factors,
):
    f32 = jnp.float32
    rows = HOURS * SECTOR // LANES
    level_cols = pltpu.VMEM((LEVELS, LANES), f32)
    per_point = pltpu.VMEM((GPB, HALF, LANES), f32)
    with jax.named_scope("pack"):
        words = pl.pallas_call(
            pack_kernel, out_shape=pltpu.VMEM((LEVELS, LANES), jnp.int32), compiler_params=SMALL
        )(
            in_hbm(thermal_anomaly.reshape(rows, LANES)),
            in_hbm(humidity_amount.reshape(rows, LANES)),
            in_hbm(slab_condensate_amount.reshape(rows, LANES)),
        )
    words = exchange(words, "slab", FIRST_SLAB)
    with jax.named_scope("prepare"):
        gas, low_gas, cloud, weight, overcast, mix = pl.pallas_call(
            prepare_kernel,
            out_shape=(
                pltpu.VMEM((KEPT, GPB, HALF, LANES), f32),
                pltpu.HBM((LEVELS - KEPT, GPB, HALF, LANES), f32),
                per_point,
                per_point,
                pltpu.VMEM((HALF, LANES), f32),
                pltpu.VMEM((2 * DISKS * COLS, PIX), jnp.bfloat16),
            ),
            compiler_params=SMALL,
        )(
            in_hbm(molecular_opacity),
            in_hbm(condensate_opacity.reshape(1, -1)),
            in_hbm(planck_quadrature_factor.reshape(1, -1)),
            in_hbm(overcast_indicator),
            in_hbm(scene_contributing_profiles),
            in_hbm(scene_interpolation_factors),
        )
    with jax.named_scope("radiate"):
        radiance = pl.pallas_call(
            radiate_kernel,
            out_shape=pltpu.VMEM((DISKS, HALF, LANES), f32),
            in_specs=[ANY if k == 2 else pl.BlockSpec() for k in range(6)],
            scratch_shapes=[
                pltpu.VMEM((LEVELS - KEPT, GPB, HALF, LANES), f32),
                level_cols,
                level_cols,
                pltpu.VMEM((LEVELS + 8, LANES), f32),
                level_cols,
                pltpu.SemaphoreType.DMA,
            ],
            compiler_params=SMALL,
        )(in_vmem(words), gas, in_hbm(low_gas), cloud, weight, overcast)
    radiance = exchange(radiance, "disk", FIRST_DISK)
    with jax.named_scope("pixels"):
        pixels = pl.pallas_call(
            pixel_kernel,
            out_shape=jax.ShapeDtypeStruct((HOURS * BANDS, PIX), f32),
            compiler_params=SMALL,
        )(in_vmem(radiance), mix)
    return pixels.reshape(HOURS, BANDS, PIX)


def solution(mesh):
    in_specs = (
        P(None, "slab", "disk"),
        P(None, "slab", "disk"),
        P(None, "slab", "disk"),
        P(None, "disk"),
        P(),
        P(),
        P(),
        P(None, ("slab", "disk")),
        P(None, ("slab", "disk")),
    )
    out_specs = P(None, None, ("slab", "disk"))
    return jax.shard_map(local, mesh=mesh, in_specs=in_specs, out_specs=out_specs, check_vma=False)
```

```python
import jax
import jax.numpy as jnp
from jax import lax
from jax.experimental import pallas as pl
from jax.experimental.pallas import tpu as pltpu
from jax.sharding import PartitionSpec as P

HOURS = 2
BANDS = 16
GPB = 7
LEVELS = 128
TAPS = 4
COLS = 32
DISKS = 4
SECTOR = 4096
PIX = 512
HALF = BANDS // 2
LANES = 128
FIRST_SLAB = 75
FIRST_DISK = 2
EARLY = 3
LOG2E = 1.4426950408889634

HUM_LOW, HUM_STEP = 0.2, 1.8 / 65535.0
CON_LOW, CON_STEP = 0.1, 1.9 / 65535.0
T4_SCALE = float(2**28)


def code16(x, low, step):
    q = ((x - low) * (1.0 / step) + 0.5).astype(jnp.int32)
    return jnp.clip(q, 0, 65535)


def swapped_group(size, first):
    return [first if i == 0 else 0 if i == first else i for i in range(size)]


def swap_rows(ref):
    if FIRST_SLAB:
        held = ref[0:1, :]
        ref[0:1, :] = ref[FIRST_SLAB : FIRST_SLAB + 1, :]
        ref[FIRST_SLAB : FIRST_SLAB + 1, :] = held


def turn(x, shift):
    return x if isinstance(shift, int) and shift == 0 else pltpu.roll(x, shift, 1)


def is_early():
    return lax.rem(lax.axis_index("slab") // 2, 8) < EARLY


def fetch(pairs, sem_ref):
    copies = [pltpu.make_async_copy(src, dst, sem_ref.at[k]) for k, (src, dst) in enumerate(pairs)]
    for copy in copies:
        copy.start()
    return copies


def pack(temp_ref, hum_ref, con_ref, copies, out_ref):
    rows = SECTOR // LANES
    lane = lax.broadcasted_iota(jnp.int32, (rows, LANES), 1) // COLS
    copies[0].wait()
    t2 = temp_ref[...] * temp_ref[...]
    t4 = (t2 * t2 * T4_SCALE).astype(jnp.int32)
    copies[1].wait()
    hum = code16(hum_ref[...], HUM_LOW, HUM_STEP)
    copies[2].wait()
    con = code16(con_ref[...], CON_LOW, CON_STEP)
    gas = (hum << 16) | con
    parts = (gas[:rows], gas[rows:], t4[:rows], t4[rows:])
    for dest in range(LANES // COLS):
        word = None
        for spot, part in enumerate(parts):
            moved = turn(part, (spot - dest) % 4 * COLS)
            word = moved if word is None else jnp.where(lane == spot, moved, word)
        out_ref[pl.ds(dest, rows, stride=LANES // COLS), :] = word
    swap_rows(out_ref)


def spread(mol_hbm, con_hbm, planck_hbm, over_hbm, gas_ref, cloud_ref, weight_ref, overcast_ref, room):
    mol_ref, con_ref, planck_ref, over_ref, sem_ref = room
    strip = lax.axis_index("slab")
    group = LANES // COLS
    block = over_hbm.at[:, pl.ds(pl.multiple_of(strip // group * LANES, LANES), LANES)]
    for copy in fetch(
        ((mol_hbm, mol_ref), (con_hbm, con_ref), (planck_hbm, planck_ref), (block, over_ref)), sem_ref
    ):
        copy.wait()
    lane = lax.broadcasted_iota(jnp.int32, (HALF, LANES), 1)
    first = lane < LANES // 2
    con = jnp.broadcast_to(con_ref[...], (HALF, con_ref.shape[1]))
    planck = jnp.broadcast_to(planck_ref[...], (HALF, planck_ref.shape[1]))
    glane = lax.broadcasted_iota(jnp.int32, con.shape, 1)
    grow = lax.broadcasted_iota(jnp.int32, con.shape, 0)

    def column(values, j):
        low = jnp.sum(jnp.where(glane == grow * GPB + j, values, 0.0), axis=1, keepdims=True)
        high = jnp.sum(
            jnp.where(glane == (grow + HALF) * GPB + j, values, 0.0), axis=1, keepdims=True
        )
        return jnp.where(
            first, jnp.broadcast_to(low, (HALF, LANES)), jnp.broadcast_to(high, (HALF, LANES))
        )

    for j in range(GPB):
        cloud_ref[j] = column(con, j) * -LOG2E
        weight_ref[j] = column(planck, j)

    overcast = None
    for spot in range(group):
        row = jnp.broadcast_to(over_ref[spot % HOURS : spot % HOURS + 1, :], (HALF, LANES))
        row = pltpu.roll(row, (spot - strip % group + group) % group * COLS, 1)
        overcast = row if overcast is None else jnp.where(lane // COLS == spot, row, overcast)
    overcast_ref[...] = overcast.astype(jnp.float32)

    span = LANES // 4
    shape = (span * HALF, LANES)
    pick = lax.broadcasted_iota(jnp.int32, shape, 1) % span == (
        lax.broadcasted_iota(jnp.int32, shape, 0) // HALF
    )
    half_of = lambda axis: lax.broadcasted_iota(jnp.int32, (LANES, LANES), axis) // (LANES // 2)
    same_half = (half_of(0) == half_of(1)).astype(jnp.float32).astype(jnp.bfloat16)

    def levels(q, _):
        for j in range(GPB):
            row = None
            for half in range(2):
                tile = mol_ref[pl.ds(half * HALF * GPB + j, HALF, stride=GPB), :] * -LOG2E
                high = tile.astype(jnp.bfloat16).astype(jnp.float32)
                for k, piece in enumerate((high, tile - high)):
                    spot = 2 * half + k
                    moved = turn(piece, (spot - q + 4) % 4 * span)
                    row = moved if row is None else jnp.where(lane // span == spot, moved, row)
            rows = jnp.broadcast_to(row[None], (span, HALF, LANES)).reshape(shape)
            rows = jnp.where(pick, rows, 0.0).astype(jnp.bfloat16)
            wide = jnp.dot(rows, same_half, preferred_element_type=jnp.float32)
            start = pl.multiple_of(q * span, span)
            gas_ref[pl.ds(start, span), j] = wide.reshape(span, HALF, LANES)
        return 0

    lax.fori_loop(0, 4, levels, 0)


def blend(source_hbm, factor_hbm, mix_ref, room):
    source_ref, factor_ref, sem_ref = room
    for copy in fetch(((source_hbm, source_ref), (factor_hbm, factor_ref)), sem_ref):
        copy.wait()
    strip_cols = DISKS * COLS
    col = lax.broadcasted_iota(jnp.int32, (strip_cols, PIX), 0)
    source = source_ref[...]
    local = source // SECTOR * COLS + source % COLS
    mix = jnp.zeros((strip_cols, PIX), jnp.float32)
    for tap in range(TAPS):
        mix = mix + jnp.where(col == local[tap : tap + 1], factor_ref[tap : tap + 1, :], 0.0)
    high = mix.astype(jnp.bfloat16)
    mix_ref[pl.ds(0, strip_cols), :] = high
    mix_ref[pl.ds(strip_cols, strip_cols), :] = (mix - high.astype(jnp.float32)).astype(jnp.bfloat16)


def pack_kernel(
    temp_hbm, hum_hbm, con_hbm, mol_hbm, cond_hbm, planck_hbm, over_hbm, source_hbm, factor_hbm,
    word_ref, gas_ref, cloud_ref, weight_ref, overcast_ref, mix_ref,
    temp_ref, hum_ref, con_ref, field_sem, *room,
):
    fields = (temp_hbm, temp_ref), (hum_hbm, hum_ref), (con_hbm, con_ref)
    pack(temp_ref, hum_ref, con_ref, fetch(fields, field_sem), word_ref)

    @pl.when(is_early())
    def _():
        spread(
            mol_hbm, cond_hbm, planck_hbm, over_hbm,
            gas_ref, cloud_ref, weight_ref, overcast_ref, room[:5],
        )
        blend(source_hbm, factor_hbm, mix_ref, room[5:])


def radiate(word_ref, gas_ref, cloud_ref, weight_ref, overcast_ref, out_ref, rows):
    hum_ref, con_ref, t4_ref, diff_ref = rows
    word = word_ref[...]
    swapped = pltpu.roll(word, LANES // 2, 1)
    first = lax.broadcasted_iota(jnp.int32, word.shape, 1) < LANES // 2
    gas = jnp.where(first, word, swapped)
    t4 = jnp.where(first, swapped, word)
    hum = lax.shift_right_logical(gas, 16)
    con = gas & 65535
    hum_ref[...] = hum.astype(jnp.float32) * HUM_STEP + HUM_LOW
    con_ref[...] = (con.astype(jnp.float32) * CON_STEP + CON_LOW) * overcast_ref[0:1, :]
    t4_ref[pl.ds(0, LEVELS), :] = t4.astype(jnp.float32) * (1.0 / T4_SCALE)
    for by_sender in (hum_ref, con_ref, t4_ref):
        swap_rows(by_sender)
    t4_ref[pl.ds(LEVELS, 1), :] = t4_ref[pl.ds(LEVELS - 1, 1), :]
    diff_ref[...] = t4_ref[pl.ds(1, LEVELS), :] - t4_ref[pl.ds(0, LEVELS), :]

    zero = jnp.zeros((HALF, LANES), jnp.float32)
    clouds = [cloud_ref[j] for j in range(GPB)]

    def step(i, carry):
        depth, total = list(carry[0]), list(carry[1])
        for k in range(8):
            level = 8 * i + k
            hum_row = hum_ref[pl.ds(level, HALF, stride=0), :]
            con_row = con_ref[pl.ds(level, HALF, stride=0), :]
            diff_row = diff_ref[pl.ds(level, HALF, stride=0), :]
            for j in range(GPB):
                depth[j] = depth[j] + (gas_ref[level, j] * hum_row + clouds[j] * con_row)
                total[j] = total[j] + diff_row * jnp.exp2(depth[j])
        return tuple(depth), tuple(total)

    _, total = lax.fori_loop(0, LEVELS // 8, step, ((zero,) * GPB, (zero,) * GPB))
    top = t4_ref[pl.ds(0, HALF, stride=0), :]
    band = zero
    for j in range(GPB):
        band = band + weight_ref[j] * (top + total[j])
    band = (band / GPB).astype(jnp.bfloat16).astype(jnp.float32)
    for owner in range(DISKS):
        out_ref[owner] = band


def radiate_kernel(
    word_ref, gas_ref, cloud_ref, weight_ref, overcast_ref, mol_hbm, cond_hbm, planck_hbm, over_hbm,
    out_ref,
    own_gas, own_cloud, own_weight, own_overcast, hum_ref, con_ref, t4_ref, diff_ref, *room,
):
    rows = hum_ref, con_ref, t4_ref, diff_ref

    @pl.when(is_early())
    def _():
        radiate(word_ref, gas_ref, cloud_ref, weight_ref, overcast_ref, out_ref, rows)

    @pl.when(jnp.logical_not(is_early()))
    def _():
        own = own_gas, own_cloud, own_weight, own_overcast
        spread(mol_hbm, cond_hbm, planck_hbm, over_hbm, *own, room)
        radiate(word_ref, *own, out_ref, rows)


def pixel_kernel(rad_ref, mix_ref, source_hbm, factor_hbm, out_ref, own_mix, *room):
    lane = lax.broadcasted_iota(jnp.int32, (HALF, LANES), 1) // COLS
    sender = swapped_group(DISKS, FIRST_DISK)
    rows = []
    for hour in range(HOURS):
        for half in range(2):
            spot = half * HOURS + hour
            row = None
            for disk in range(DISKS):
                moved = turn(rad_ref[sender.index(disk)], (disk - spot) % 4 * COLS)
                row = moved if row is None else jnp.where(lane == disk, moved, row)
            rows.append(row)
    rad = jnp.concatenate(rows, axis=0).astype(jnp.bfloat16)
    rad = jnp.concatenate([rad, rad], axis=1)

    @pl.when(is_early())
    def _():
        out_ref[...] = jnp.dot(rad, mix_ref[...], preferred_element_type=jnp.float32)

    @pl.when(jnp.logical_not(is_early()))
    def _():
        blend(source_hbm, factor_hbm, own_mix, room)
        out_ref[...] = jnp.dot(rad, own_mix[...], preferred_element_type=jnp.float32)


ANY = pl.BlockSpec(memory_space=pl.ANY)
WHOLE = pl.BlockSpec(memory_space=pltpu.VMEM)
SMALL = pltpu.CompilerParams(vmem_limit_bytes=16 << 20)


def in_vmem(x):
    return pltpu.with_memory_space_constraint(x, pltpu.VMEM)


def in_hbm(x):
    return pltpu.with_memory_space_constraint(x, pltpu.HBM)


def exchange(x, axis, first):
    group = swapped_group(lax.axis_size(axis), first)
    return lax.all_to_all(x, axis, 0, 0, axis_index_groups=[group], tiled=True)


def local(
    thermal_anomaly,
    humidity_amount,
    slab_condensate_amount,
    overcast_indicator,
    molecular_opacity,
    condensate_opacity,
    planck_quadrature_factor,
    scene_contributing_profiles,
    scene_interpolation_factors,
):
    f32 = jnp.float32
    rows = HOURS * SECTOR // LANES
    field = pltpu.VMEM((rows, LANES), f32)
    level_cols = pltpu.VMEM((LEVELS, LANES), f32)
    per_point = pltpu.VMEM((GPB, HALF, LANES), f32)
    prepared = [
        pltpu.VMEM((LEVELS, GPB, HALF, LANES), f32),
        per_point,
        per_point,
        pltpu.VMEM((HALF, LANES), f32),
    ]
    mixed = pltpu.VMEM((2 * DISKS * COLS, PIX), jnp.bfloat16)
    points = condensate_opacity.shape[0]
    spread_room = [
        pltpu.VMEM((points, LEVELS), f32),
        pltpu.VMEM((1, points), f32),
        pltpu.VMEM((1, points), f32),
        pltpu.VMEM((HOURS, LANES), jnp.int32),
        pltpu.SemaphoreType.DMA((4,)),
    ]
    blend_room = [
        pltpu.VMEM((TAPS, PIX), jnp.int32),
        pltpu.VMEM((TAPS, PIX), f32),
        pltpu.SemaphoreType.DMA((2,)),
    ]
    opacities = [
        in_hbm(molecular_opacity),
        in_hbm(condensate_opacity.reshape(1, -1)),
        in_hbm(planck_quadrature_factor.reshape(1, -1)),
        in_hbm(overcast_indicator),
    ]
    scene = [in_hbm(scene_contributing_profiles), in_hbm(scene_interpolation_factors)]
    with jax.named_scope("pack"):
        words, *ready, mix = pl.pallas_call(
            pack_kernel,
            out_shape=(pltpu.VMEM((LEVELS, LANES), jnp.int32), *prepared, mixed),
            in_specs=[ANY] * 9,
            out_specs=[WHOLE] * 6,
            scratch_shapes=[field] * 3 + [pltpu.SemaphoreType.DMA((3,))] + spread_room + blend_room,
            compiler_params=SMALL,
        )(
            in_hbm(thermal_anomaly.reshape(rows, LANES)),
            in_hbm(humidity_amount.reshape(rows, LANES)),
            in_hbm(slab_condensate_amount.reshape(rows, LANES)),
            *opacities,
            *scene,
        )
    words = exchange(words, "slab", FIRST_SLAB)
    with jax.named_scope("radiate"):
        radiance = pl.pallas_call(
            radiate_kernel,
            out_shape=pltpu.VMEM((DISKS, HALF, LANES), f32),
            in_specs=[WHOLE] * 5 + [ANY] * 4,
            out_specs=WHOLE,
            scratch_shapes=prepared
            + [level_cols, level_cols, pltpu.VMEM((LEVELS + 8, LANES), f32), level_cols]
            + spread_room,
            compiler_params=SMALL,
        )(in_vmem(words), *ready, *opacities)
    radiance = exchange(radiance, "disk", FIRST_DISK)
    with jax.named_scope("pixels"):
        pixels = pl.pallas_call(
            pixel_kernel,
            out_shape=jax.ShapeDtypeStruct((HOURS * BANDS, PIX), f32),
            in_specs=[WHOLE] * 2 + [ANY] * 2,
            scratch_shapes=[mixed] + blend_room,
            compiler_params=SMALL,
        )(in_vmem(radiance), mix, *scene)
    return pixels.reshape(HOURS, BANDS, PIX)


def solution(mesh):
    in_specs = (
        P(None, "slab", "disk"),
        P(None, "slab", "disk"),
        P(None, "slab", "disk"),
        P(None, "disk"),
        P(),
        P(),
        P(),
        P(None, ("slab", "disk")),
        P(None, ("slab", "disk")),
    )
    out_specs = P(None, None, ("slab", "disk"))
    return jax.shard_map(local, mesh=mesh, in_specs=in_specs, out_specs=out_specs, check_vma=False)
```

```python
import jax
import jax.numpy as jnp
from jax import lax
from jax.experimental import pallas as pl
from jax.experimental.pallas import tpu as pltpu
from jax.sharding import PartitionSpec as P

HOURS = 2
BANDS = 16
GPB = 7
LEVELS = 128
TAPS = 4
COLS = 32
DISKS = 4
SECTOR = 4096
PIX = 512
HALF = BANDS // 2
LANES = 128
FIRST_SLAB = 75
FIRST_DISK = 2
EARLY = 3
STEP = 32
LOG2E = 1.4426950408889634

HUM_LOW, HUM_STEP = 0.2, 1.8 / 65535.0
CON_LOW, CON_STEP = 0.1, 1.9 / 65535.0
T4_SCALE = float(2**28)


def code16(x, low, step):
    q = ((x - low) * (1.0 / step) + 0.5).astype(jnp.int32)
    return jnp.clip(q, 0, 65535)


def swapped_group(size, first):
    return [first if i == 0 else 0 if i == first else i for i in range(size)]


def swap_rows(ref):
    if FIRST_SLAB:
        held = ref[0:1, :]
        ref[0:1, :] = ref[FIRST_SLAB : FIRST_SLAB + 1, :]
        ref[FIRST_SLAB : FIRST_SLAB + 1, :] = held


def turn(x, shift):
    return x if isinstance(shift, int) and shift == 0 else pltpu.roll(x, shift, 1)


def is_early():
    return lax.rem(lax.axis_index("slab") // 2, 8) < EARLY


def fetch(pairs, sem_ref):
    copies = [pltpu.make_async_copy(src, dst, sem_ref.at[k]) for k, (src, dst) in enumerate(pairs)]
    for copy in copies:
        copy.start()
    return copies


def pack(temp_ref, hum_ref, con_ref, copies, out_ref):
    rows = SECTOR // LANES
    lane = lax.broadcasted_iota(jnp.int32, (rows, LANES), 1) // COLS
    copies[0].wait()
    t2 = temp_ref[...] * temp_ref[...]
    t4 = (t2 * t2 * T4_SCALE).astype(jnp.int32)
    copies[1].wait()
    hum = code16(hum_ref[...], HUM_LOW, HUM_STEP)
    copies[2].wait()
    con = code16(con_ref[...], CON_LOW, CON_STEP)
    gas = (hum << 16) | con
    parts = (gas[:rows], gas[rows:], t4[:rows], t4[rows:])
    for dest in range(LANES // COLS):
        word = None
        for spot, part in enumerate(parts):
            moved = turn(part, (spot - dest) % 4 * COLS)
            word = moved if word is None else jnp.where(lane == spot, moved, word)
        out_ref[pl.ds(dest, rows, stride=LANES // COLS), :] = word
    swap_rows(out_ref)


def spread(mol_hbm, con_hbm, planck_hbm, over_hbm, gas_ref, cloud_ref, start_ref, weight_ref, overcast_ref, room):
    mol_ref, con_ref, planck_ref, over_ref, sem_ref = room
    strip = lax.axis_index("slab")
    group = LANES // COLS
    block = over_hbm.at[:, pl.ds(pl.multiple_of(strip // group * LANES, LANES), LANES)]
    for copy in fetch(
        ((mol_hbm, mol_ref), (con_hbm, con_ref), (planck_hbm, planck_ref), (block, over_ref)), sem_ref
    ):
        copy.wait()
    lane = lax.broadcasted_iota(jnp.int32, (HALF, LANES), 1)
    first = lane < LANES // 2
    con = jnp.broadcast_to(con_ref[...], (HALF, con_ref.shape[1]))
    planck = jnp.broadcast_to(planck_ref[...], (HALF, planck_ref.shape[1]))
    glane = lax.broadcasted_iota(jnp.int32, con.shape, 1)
    grow = lax.broadcasted_iota(jnp.int32, con.shape, 0)

    def column(values, j):
        low = jnp.sum(jnp.where(glane == grow * GPB + j, values, 0.0), axis=1, keepdims=True)
        high = jnp.sum(
            jnp.where(glane == (grow + HALF) * GPB + j, values, 0.0), axis=1, keepdims=True
        )
        return jnp.where(
            first, jnp.broadcast_to(low, (HALF, LANES)), jnp.broadcast_to(high, (HALF, LANES))
        )

    for j in range(GPB):
        cloud_ref[j] = column(con, j) * -LOG2E
        weight = column(planck, j)
        start_ref[j] = jnp.log(weight) * LOG2E
        total = weight if j == 0 else total + weight
    weight_ref[...] = total

    overcast = None
    for spot in range(group):
        row = jnp.broadcast_to(over_ref[spot % HOURS : spot % HOURS + 1, :], (HALF, LANES))
        row = pltpu.roll(row, (spot - strip % group + group) % group * COLS, 1)
        overcast = row if overcast is None else jnp.where(lane // COLS == spot, row, overcast)
    overcast_ref[...] = overcast.astype(jnp.float32)

    span = LANES // 4
    shape = (span * HALF, LANES)
    pick = lax.broadcasted_iota(jnp.int32, shape, 1) % span == (
        lax.broadcasted_iota(jnp.int32, shape, 0) // HALF
    )
    half_of = lambda axis: lax.broadcasted_iota(jnp.int32, (LANES, LANES), axis) // (LANES // 2)
    same_half = (half_of(0) == half_of(1)).astype(jnp.float32).astype(jnp.bfloat16)

    def levels(q, _):
        for j in range(GPB):
            row = None
            for half in range(2):
                tile = mol_ref[pl.ds(half * HALF * GPB + j, HALF, stride=GPB), :] * -LOG2E
                high = tile.astype(jnp.bfloat16).astype(jnp.float32)
                for k, piece in enumerate((high, tile - high)):
                    spot = 2 * half + k
                    moved = turn(piece, (spot - q + 4) % 4 * span)
                    row = moved if row is None else jnp.where(lane // span == spot, moved, row)
            rows = jnp.broadcast_to(row[None], (span, HALF, LANES)).reshape(shape)
            rows = jnp.where(pick, rows, 0.0).astype(jnp.bfloat16)
            wide = jnp.dot(rows, same_half, preferred_element_type=jnp.float32)
            start = pl.multiple_of(q * span, span)
            gas_ref[pl.ds(start, span), j] = wide.reshape(span, HALF, LANES)
        return 0

    lax.fori_loop(0, 4, levels, 0)


def blend(source_hbm, factor_hbm, mix_ref, room):
    source_ref, factor_ref, sem_ref = room
    for copy in fetch(((source_hbm, source_ref), (factor_hbm, factor_ref)), sem_ref):
        copy.wait()
    strip_cols = DISKS * COLS
    col = lax.broadcasted_iota(jnp.int32, (strip_cols, PIX), 0)
    source = source_ref[...]
    local = source // SECTOR * COLS + source % COLS
    mix = jnp.zeros((strip_cols, PIX), jnp.float32)
    for tap in range(TAPS):
        mix = mix + jnp.where(col == local[tap : tap + 1], factor_ref[tap : tap + 1, :], 0.0)
    high = mix.astype(jnp.bfloat16)
    mix_ref[pl.ds(0, strip_cols), :] = high
    mix_ref[pl.ds(strip_cols, strip_cols), :] = (mix - high.astype(jnp.float32)).astype(jnp.bfloat16)


def pack_kernel(
    temp_hbm, hum_hbm, con_hbm, mol_hbm, cond_hbm, planck_hbm, over_hbm, source_hbm, factor_hbm,
    word_ref, gas_ref, cloud_ref, start_ref, weight_ref, overcast_ref, mix_ref,
    temp_ref, hum_ref, con_ref, field_sem, *room,
):
    fields = (temp_hbm, temp_ref), (hum_hbm, hum_ref), (con_hbm, con_ref)
    pack(temp_ref, hum_ref, con_ref, fetch(fields, field_sem), word_ref)

    @pl.when(is_early())
    def _():
        spread(
            mol_hbm, cond_hbm, planck_hbm, over_hbm,
            gas_ref, cloud_ref, start_ref, weight_ref, overcast_ref, room[:5],
        )
        blend(source_hbm, factor_hbm, mix_ref, room[5:])


def radiate(word_ref, gas_ref, cloud_ref, start_ref, weight_ref, overcast_ref, out_ref, rows):
    hum_ref, con_ref, t4_ref, diff_ref = rows
    word = word_ref[...]
    swapped = pltpu.roll(word, LANES // 2, 1)
    first = lax.broadcasted_iota(jnp.int32, word.shape, 1) < LANES // 2
    gas = jnp.where(first, word, swapped)
    t4 = jnp.where(first, swapped, word)
    hum = lax.shift_right_logical(gas, 16)
    con = gas & 65535
    hum_ref[...] = hum.astype(jnp.float32) * HUM_STEP + HUM_LOW
    con_ref[...] = (con.astype(jnp.float32) * CON_STEP + CON_LOW) * overcast_ref[0:1, :]
    t4_ref[pl.ds(0, LEVELS), :] = t4.astype(jnp.float32) * (1.0 / T4_SCALE)
    for by_sender in (hum_ref, con_ref, t4_ref):
        swap_rows(by_sender)
    t4_ref[pl.ds(LEVELS, 1), :] = t4_ref[pl.ds(LEVELS - 1, 1), :]
    diff_ref[...] = t4_ref[pl.ds(1, LEVELS), :] - t4_ref[pl.ds(0, LEVELS), :]

    clouds = [cloud_ref[j] for j in range(GPB)]

    def step(i, carry):
        depth, total = list(carry[0]), carry[1]
        for k in range(STEP):
            level = STEP * i + k
            hum_row = hum_ref[pl.ds(level, HALF, stride=0), :]
            con_row = con_ref[pl.ds(level, HALF, stride=0), :]
            diff_row = diff_ref[pl.ds(level, HALF, stride=0), :]
            for j in range(GPB):
                depth[j] = depth[j] + (gas_ref[level, j] * hum_row + clouds[j] * con_row)
            seen = [jnp.exp2(x) for x in depth]
            while len(seen) > 1:
                seen = [a + b for a, b in zip(seen[::2], seen[1::2])] + seen[len(seen) // 2 * 2 :]
            total = total + diff_row * seen[0]
        return tuple(depth), total

    starts = tuple(start_ref[j] for j in range(GPB))
    _, total = lax.fori_loop(0, LEVELS // STEP, step, (starts, jnp.zeros((HALF, LANES), jnp.float32)))
    top = t4_ref[pl.ds(0, HALF, stride=0), :]
    band = ((weight_ref[...] * top + total) / GPB).astype(jnp.bfloat16)
    for owner in range(DISKS):
        out_ref[owner] = band


def radiate_kernel(
    word_ref, gas_ref, cloud_ref, start_ref, weight_ref, overcast_ref, mol_hbm, cond_hbm, planck_hbm, over_hbm,
    out_ref,
    own_gas, own_cloud, own_start, own_weight, own_overcast, hum_ref, con_ref, t4_ref, diff_ref, *room,
):
    rows = hum_ref, con_ref, t4_ref, diff_ref

    @pl.when(is_early())
    def _():
        radiate(word_ref, gas_ref, cloud_ref, start_ref, weight_ref, overcast_ref, out_ref, rows)

    @pl.when(jnp.logical_not(is_early()))
    def _():
        own = own_gas, own_cloud, own_start, own_weight, own_overcast
        spread(mol_hbm, cond_hbm, planck_hbm, over_hbm, *own, room)
        radiate(word_ref, *own, out_ref, rows)


def pixel_kernel(rad_ref, mix_ref, source_hbm, factor_hbm, out_ref, own_mix, *room):
    lane = lax.broadcasted_iota(jnp.int32, (HALF, LANES), 1) // COLS
    sender = swapped_group(DISKS, FIRST_DISK)
    rows = []
    for hour in range(HOURS):
        for half in range(2):
            spot = half * HOURS + hour
            row = None
            for disk in range(DISKS):
                moved = turn(rad_ref[sender.index(disk)].astype(jnp.float32), (disk - spot) % 4 * COLS)
                row = moved if row is None else jnp.where(lane == disk, moved, row)
            rows.append(row)
    rad = jnp.concatenate(rows, axis=0).astype(jnp.bfloat16)
    rad = jnp.concatenate([rad, rad], axis=1)

    @pl.when(is_early())
    def _():
        out_ref[...] = jnp.dot(rad, mix_ref[...], preferred_element_type=jnp.float32)

    @pl.when(jnp.logical_not(is_early()))
    def _():
        blend(source_hbm, factor_hbm, own_mix, room)
        out_ref[...] = jnp.dot(rad, own_mix[...], preferred_element_type=jnp.float32)


ANY = pl.BlockSpec(memory_space=pl.ANY)
WHOLE = pl.BlockSpec(memory_space=pltpu.VMEM)
SMALL = pltpu.CompilerParams(vmem_limit_bytes=16 << 20)


def in_vmem(x):
    return pltpu.with_memory_space_constraint(x, pltpu.VMEM)


def in_hbm(x):
    return pltpu.with_memory_space_constraint(x, pltpu.HBM)


def exchange(x, axis, first):
    group = swapped_group(lax.axis_size(axis), first)
    return lax.all_to_all(x, axis, 0, 0, axis_index_groups=[group], tiled=True)


def local(
    thermal_anomaly,
    humidity_amount,
    slab_condensate_amount,
    overcast_indicator,
    molecular_opacity,
    condensate_opacity,
    planck_quadrature_factor,
    scene_contributing_profiles,
    scene_interpolation_factors,
):
    f32 = jnp.float32
    rows = HOURS * SECTOR // LANES
    field = pltpu.VMEM((rows, LANES), f32)
    level_cols = pltpu.VMEM((LEVELS, LANES), f32)
    per_point = pltpu.VMEM((GPB, HALF, LANES), f32)
    prepared = [
        pltpu.VMEM((LEVELS, GPB, HALF, LANES), f32),
        per_point,
        per_point,
        pltpu.VMEM((HALF, LANES), f32),
        pltpu.VMEM((HALF, LANES), f32),
    ]
    mixed = pltpu.VMEM((2 * DISKS * COLS, PIX), jnp.bfloat16)
    points = condensate_opacity.shape[0]
    spread_room = [
        pltpu.VMEM((points, LEVELS), f32),
        pltpu.VMEM((1, points), f32),
        pltpu.VMEM((1, points), f32),
        pltpu.VMEM((HOURS, LANES), jnp.int32),
        pltpu.SemaphoreType.DMA((4,)),
    ]
    blend_room = [
        pltpu.VMEM((TAPS, PIX), jnp.int32),
        pltpu.VMEM((TAPS, PIX), f32),
        pltpu.SemaphoreType.DMA((2,)),
    ]
    opacities = [
        in_hbm(molecular_opacity),
        in_hbm(condensate_opacity.reshape(1, -1)),
        in_hbm(planck_quadrature_factor.reshape(1, -1)),
        in_hbm(overcast_indicator),
    ]
    scene = [in_hbm(scene_contributing_profiles), in_hbm(scene_interpolation_factors)]
    with jax.named_scope("pack"):
        words, *ready, mix = pl.pallas_call(
            pack_kernel,
            out_shape=(pltpu.VMEM((LEVELS, LANES), jnp.int32), *prepared, mixed),
            in_specs=[ANY] * 9,
            out_specs=[WHOLE] * 7,
            scratch_shapes=[field] * 3 + [pltpu.SemaphoreType.DMA((3,))] + spread_room + blend_room,
            compiler_params=SMALL,
        )(
            in_hbm(thermal_anomaly.reshape(rows, LANES)),
            in_hbm(humidity_amount.reshape(rows, LANES)),
            in_hbm(slab_condensate_amount.reshape(rows, LANES)),
            *opacities,
            *scene,
        )
    words = exchange(words, "slab", FIRST_SLAB)
    with jax.named_scope("radiate"):
        radiance = pl.pallas_call(
            radiate_kernel,
            out_shape=pltpu.VMEM((DISKS, HALF, LANES), jnp.bfloat16),
            in_specs=[WHOLE] * 6 + [ANY] * 4,
            out_specs=WHOLE,
            scratch_shapes=prepared
            + [level_cols, level_cols, pltpu.VMEM((LEVELS + 8, LANES), f32), level_cols]
            + spread_room,
            compiler_params=SMALL,
        )(in_vmem(words), *ready, *opacities)
    radiance = exchange(radiance, "disk", FIRST_DISK)
    with jax.named_scope("pixels"):
        pixels = pl.pallas_call(
            pixel_kernel,
            out_shape=jax.ShapeDtypeStruct((HOURS * BANDS, PIX), f32),
            in_specs=[WHOLE] * 2 + [ANY] * 2,
            scratch_shapes=[mixed] + blend_room,
            compiler_params=SMALL,
        )(in_vmem(radiance), mix, *scene)
    return pixels.reshape(HOURS, BANDS, PIX)


def solution(mesh):
    in_specs = (
        P(None, "slab", "disk"),
        P(None, "slab", "disk"),
        P(None, "slab", "disk"),
        P(None, "disk"),
        P(),
        P(),
        P(),
        P(None, ("slab", "disk")),
        P(None, ("slab", "disk")),
    )
    out_specs = P(None, None, ("slab", "disk"))
    return jax.shard_map(local, mesh=mesh, in_specs=in_specs, out_specs=out_specs, check_vma=False)
```

```python
import jax
import jax.numpy as jnp
from jax import lax
from jax.experimental import pallas as pl
from jax.experimental.pallas import tpu as pltpu
from jax.sharding import PartitionSpec as P

HOURS = 2
BANDS = 16
GPB = 7
LEVELS = 128
TAPS = 4
COLS = 32
DISKS = 4
SECTOR = 4096
PIX = 512
HALF = BANDS // 2
LANES = 128
FIRST_SLAB = 75
FIRST_DISK = 2
EARLY = 3
STEP = 128
LOG2E = 1.4426950408889634

HUM_LOW, HUM_STEP = 0.2, 1.8 / 65535.0
CON_LOW, CON_STEP = 0.1, 1.9 / 65535.0
T4_SCALE = float(2**28)


def code16(x, low, step):
    q = ((x - low) * (1.0 / step) + 0.5).astype(jnp.int32)
    return jnp.clip(q, 0, 65535)


def swapped_group(size, first):
    return [first if i == 0 else 0 if i == first else i for i in range(size)]


def swap_rows(ref):
    if FIRST_SLAB:
        held = ref[0:1, :]
        ref[0:1, :] = ref[FIRST_SLAB : FIRST_SLAB + 1, :]
        ref[FIRST_SLAB : FIRST_SLAB + 1, :] = held


def turn(x, shift):
    return x if isinstance(shift, int) and shift == 0 else pltpu.roll(x, shift, 1)


def is_early():
    return lax.rem(lax.axis_index("slab") // 2, 8) < EARLY


def fetch(pairs, sem_ref):
    copies = [pltpu.make_async_copy(src, dst, sem_ref.at[k]) for k, (src, dst) in enumerate(pairs)]
    for copy in copies:
        copy.start()
    return copies


def pack(temp_ref, hum_ref, con_ref, copies, out_ref):
    rows = SECTOR // LANES
    lane = lax.broadcasted_iota(jnp.int32, (rows, LANES), 1) // COLS
    copies[0].wait()
    t2 = temp_ref[...] * temp_ref[...]
    t4 = (t2 * t2 * T4_SCALE).astype(jnp.int32)
    copies[1].wait()
    hum = code16(hum_ref[...], HUM_LOW, HUM_STEP)
    copies[2].wait()
    con = code16(con_ref[...], CON_LOW, CON_STEP)
    gas = (hum << 16) | con
    parts = (gas[:rows], gas[rows:], t4[:rows], t4[rows:])
    for dest in range(LANES // COLS):
        word = None
        for spot, part in enumerate(parts):
            moved = turn(part, (spot - dest) % 4 * COLS)
            word = moved if word is None else jnp.where(lane == spot, moved, word)
        out_ref[pl.ds(dest, rows, stride=LANES // COLS), :] = word
    swap_rows(out_ref)


def spread(mol_hbm, con_hbm, planck_hbm, over_hbm, gas_ref, cloud_ref, start_ref, weight_ref, overcast_ref, room):
    mol_ref, con_ref, planck_ref, over_ref, sem_ref = room
    strip = lax.axis_index("slab")
    group = LANES // COLS
    block = over_hbm.at[:, pl.ds(pl.multiple_of(strip // group * LANES, LANES), LANES)]
    for copy in fetch(
        ((mol_hbm, mol_ref), (con_hbm, con_ref), (planck_hbm, planck_ref), (block, over_ref)), sem_ref
    ):
        copy.wait()
    lane = lax.broadcasted_iota(jnp.int32, (HALF, LANES), 1)
    first = lane < LANES // 2
    con = jnp.broadcast_to(con_ref[...], (HALF, con_ref.shape[1]))
    planck = jnp.broadcast_to(planck_ref[...], (HALF, planck_ref.shape[1]))
    glane = lax.broadcasted_iota(jnp.int32, con.shape, 1)
    grow = lax.broadcasted_iota(jnp.int32, con.shape, 0)

    def column(values, j):
        low = jnp.sum(jnp.where(glane == grow * GPB + j, values, 0.0), axis=1, keepdims=True)
        high = jnp.sum(
            jnp.where(glane == (grow + HALF) * GPB + j, values, 0.0), axis=1, keepdims=True
        )
        return jnp.where(
            first, jnp.broadcast_to(low, (HALF, LANES)), jnp.broadcast_to(high, (HALF, LANES))
        )

    for j in range(GPB):
        cloud_ref[j] = column(con, j) * -LOG2E
        weight = column(planck, j)
        start_ref[j] = jnp.log(weight) * LOG2E
        total = weight if j == 0 else total + weight
    weight_ref[...] = total

    overcast = None
    for spot in range(group):
        row = jnp.broadcast_to(over_ref[spot % HOURS : spot % HOURS + 1, :], (HALF, LANES))
        row = pltpu.roll(row, (spot - strip % group + group) % group * COLS, 1)
        overcast = row if overcast is None else jnp.where(lane // COLS == spot, row, overcast)
    overcast_ref[...] = overcast.astype(jnp.float32)

    span = LANES // 4
    shape = (span * HALF, LANES)
    pick = lax.broadcasted_iota(jnp.int32, shape, 1) % span == (
        lax.broadcasted_iota(jnp.int32, shape, 0) // HALF
    )
    half_of = lambda axis: lax.broadcasted_iota(jnp.int32, (LANES, LANES), axis) // (LANES // 2)
    same_half = (half_of(0) == half_of(1)).astype(jnp.float32).astype(jnp.bfloat16)

    def levels(q, _):
        for j in range(GPB):
            row = None
            for half in range(2):
                tile = mol_ref[pl.ds(half * HALF * GPB + j, HALF, stride=GPB), :] * -LOG2E
                high = tile.astype(jnp.bfloat16).astype(jnp.float32)
                for k, piece in enumerate((high, tile - high)):
                    spot = 2 * half + k
                    moved = turn(piece, (spot - q + 4) % 4 * span)
                    row = moved if row is None else jnp.where(lane // span == spot, moved, row)
            rows = jnp.broadcast_to(row[None], (span, HALF, LANES)).reshape(shape)
            rows = jnp.where(pick, rows, 0.0).astype(jnp.bfloat16)
            wide = jnp.dot(rows, same_half, preferred_element_type=jnp.float32)
            start = pl.multiple_of(q * span, span)
            gas_ref[pl.ds(start, span), j] = wide.reshape(span, HALF, LANES)
        return 0

    lax.fori_loop(0, 4, levels, 0)


def blend(source_hbm, factor_hbm, mix_ref, room):
    source_ref, factor_ref, sem_ref = room
    for copy in fetch(((source_hbm, source_ref), (factor_hbm, factor_ref)), sem_ref):
        copy.wait()
    strip_cols = DISKS * COLS
    col = lax.broadcasted_iota(jnp.int32, (strip_cols, PIX), 0)
    source = source_ref[...]
    local = source // SECTOR * COLS + source % COLS
    mix = jnp.zeros((strip_cols, PIX), jnp.float32)
    for tap in range(TAPS):
        mix = mix + jnp.where(col == local[tap : tap + 1], factor_ref[tap : tap + 1, :], 0.0)
    high = mix.astype(jnp.bfloat16)
    mix_ref[pl.ds(0, strip_cols), :] = high
    mix_ref[pl.ds(strip_cols, strip_cols), :] = (mix - high.astype(jnp.float32)).astype(jnp.bfloat16)


def pack_kernel(
    temp_hbm, hum_hbm, con_hbm, mol_hbm, cond_hbm, planck_hbm, over_hbm, source_hbm, factor_hbm,
    word_ref, gas_ref, cloud_ref, start_ref, weight_ref, overcast_ref, mix_ref,
    temp_ref, hum_ref, con_ref, field_sem, *room,
):
    fields = (temp_hbm, temp_ref), (hum_hbm, hum_ref), (con_hbm, con_ref)
    pack(temp_ref, hum_ref, con_ref, fetch(fields, field_sem), word_ref)

    @pl.when(is_early())
    def _():
        spread(
            mol_hbm, cond_hbm, planck_hbm, over_hbm,
            gas_ref, cloud_ref, start_ref, weight_ref, overcast_ref, room[:5],
        )
        blend(source_hbm, factor_hbm, mix_ref, room[5:])


def radiate(word_ref, gas_ref, cloud_ref, start_ref, weight_ref, overcast_ref, out_ref, rows):
    hum_ref, con_ref, t4_ref, diff_ref = rows
    word = word_ref[...]
    swapped = pltpu.roll(word, LANES // 2, 1)
    first = lax.broadcasted_iota(jnp.int32, word.shape, 1) < LANES // 2
    gas = jnp.where(first, word, swapped)
    t4 = jnp.where(first, swapped, word)
    hum = lax.shift_right_logical(gas, 16)
    con = gas & 65535
    hum_ref[...] = hum.astype(jnp.float32) * HUM_STEP + HUM_LOW
    con_ref[...] = (con.astype(jnp.float32) * CON_STEP + CON_LOW) * overcast_ref[0:1, :]
    t4_ref[pl.ds(0, LEVELS), :] = t4.astype(jnp.float32) * (1.0 / T4_SCALE)
    for by_sender in (hum_ref, con_ref, t4_ref):
        swap_rows(by_sender)
    t4_ref[pl.ds(LEVELS, 1), :] = t4_ref[pl.ds(LEVELS - 1, 1), :]
    diff_ref[...] = t4_ref[pl.ds(1, LEVELS), :] - t4_ref[pl.ds(0, LEVELS), :]

    clouds = [cloud_ref[j] for j in range(GPB)]

    def step(i, carry):
        depth, total = list(carry[0]), carry[1]
        for k in range(STEP):
            level = STEP * i + k
            hum_row = hum_ref[pl.ds(level, HALF, stride=0), :]
            con_row = con_ref[pl.ds(level, HALF, stride=0), :]
            diff_row = diff_ref[pl.ds(level, HALF, stride=0), :]
            for j in range(GPB):
                depth[j] = depth[j] + (gas_ref[level, j] * hum_row + clouds[j] * con_row)
            seen = [jnp.exp2(x) for x in depth]
            while len(seen) > 1:
                seen = [a + b for a, b in zip(seen[::2], seen[1::2])] + seen[len(seen) // 2 * 2 :]
            total = total + diff_row * seen[0]
        return tuple(depth), total

    starts = tuple(start_ref[j] for j in range(GPB))
    _, total = lax.fori_loop(0, LEVELS // STEP, step, (starts, jnp.zeros((HALF, LANES), jnp.float32)))
    top = t4_ref[pl.ds(0, HALF, stride=0), :]
    band = ((weight_ref[...] * top + total) / GPB).astype(jnp.bfloat16)
    for owner in range(DISKS):
        out_ref[owner] = band


def radiate_kernel(
    word_ref, gas_ref, cloud_ref, start_ref, weight_ref, overcast_ref, mol_hbm, cond_hbm, planck_hbm, over_hbm,
    out_ref,
    own_gas, own_cloud, own_start, own_weight, own_overcast, hum_ref, con_ref, t4_ref, diff_ref, *room,
):
    rows = hum_ref, con_ref, t4_ref, diff_ref

    @pl.when(is_early())
    def _():
        radiate(word_ref, gas_ref, cloud_ref, start_ref, weight_ref, overcast_ref, out_ref, rows)

    @pl.when(jnp.logical_not(is_early()))
    def _():
        own = own_gas, own_cloud, own_start, own_weight, own_overcast
        spread(mol_hbm, cond_hbm, planck_hbm, over_hbm, *own, room)
        radiate(word_ref, *own, out_ref, rows)


def pixel_kernel(rad_ref, mix_ref, source_hbm, factor_hbm, out_ref, own_mix, *room):
    lane = lax.broadcasted_iota(jnp.int32, (HALF, LANES), 1) // COLS
    sender = swapped_group(DISKS, FIRST_DISK)
    rows = []
    for hour in range(HOURS):
        for half in range(2):
            spot = half * HOURS + hour
            row = None
            for disk in range(DISKS):
                moved = turn(rad_ref[sender.index(disk)].astype(jnp.float32), (disk - spot) % 4 * COLS)
                row = moved if row is None else jnp.where(lane == disk, moved, row)
            rows.append(row)
    rad = jnp.concatenate(rows, axis=0).astype(jnp.bfloat16)
    rad = jnp.concatenate([rad, rad], axis=1)

    @pl.when(is_early())
    def _():
        out_ref[...] = jnp.dot(rad, mix_ref[...], preferred_element_type=jnp.float32)

    @pl.when(jnp.logical_not(is_early()))
    def _():
        blend(source_hbm, factor_hbm, own_mix, room)
        out_ref[...] = jnp.dot(rad, own_mix[...], preferred_element_type=jnp.float32)


ANY = pl.BlockSpec(memory_space=pl.ANY)
WHOLE = pl.BlockSpec(memory_space=pltpu.VMEM)
SMALL = pltpu.CompilerParams(vmem_limit_bytes=16 << 20)


def in_vmem(x):
    return pltpu.with_memory_space_constraint(x, pltpu.VMEM)


def in_hbm(x):
    return pltpu.with_memory_space_constraint(x, pltpu.HBM)


def exchange(x, axis, first):
    group = swapped_group(lax.axis_size(axis), first)
    return lax.all_to_all(x, axis, 0, 0, axis_index_groups=[group], tiled=True)


def local(
    thermal_anomaly,
    humidity_amount,
    slab_condensate_amount,
    overcast_indicator,
    molecular_opacity,
    condensate_opacity,
    planck_quadrature_factor,
    scene_contributing_profiles,
    scene_interpolation_factors,
):
    f32 = jnp.float32
    rows = HOURS * SECTOR // LANES
    field = pltpu.VMEM((rows, LANES), f32)
    level_cols = pltpu.VMEM((LEVELS, LANES), f32)
    per_point = pltpu.VMEM((GPB, HALF, LANES), f32)
    prepared = [
        pltpu.VMEM((LEVELS, GPB, HALF, LANES), f32),
        per_point,
        per_point,
        pltpu.VMEM((HALF, LANES), f32),
        pltpu.VMEM((HALF, LANES), f32),
    ]
    mixed = pltpu.VMEM((2 * DISKS * COLS, PIX), jnp.bfloat16)
    points = condensate_opacity.shape[0]
    spread_room = [
        pltpu.VMEM((points, LEVELS), f32),
        pltpu.VMEM((1, points), f32),
        pltpu.VMEM((1, points), f32),
        pltpu.VMEM((HOURS, LANES), jnp.int32),
        pltpu.SemaphoreType.DMA((4,)),
    ]
    blend_room = [
        pltpu.VMEM((TAPS, PIX), jnp.int32),
        pltpu.VMEM((TAPS, PIX), f32),
        pltpu.SemaphoreType.DMA((2,)),
    ]
    opacities = [
        in_hbm(molecular_opacity),
        in_hbm(condensate_opacity.reshape(1, -1)),
        in_hbm(planck_quadrature_factor.reshape(1, -1)),
        in_hbm(overcast_indicator),
    ]
    scene = [in_hbm(scene_contributing_profiles), in_hbm(scene_interpolation_factors)]
    with jax.named_scope("pack"):
        words, *ready, mix = pl.pallas_call(
            pack_kernel,
            out_shape=(pltpu.VMEM((LEVELS, LANES), jnp.int32), *prepared, mixed),
            in_specs=[ANY] * 9,
            out_specs=[WHOLE] * 7,
            scratch_shapes=[field] * 3 + [pltpu.SemaphoreType.DMA((3,))] + spread_room + blend_room,
            compiler_params=SMALL,
        )(
            in_hbm(thermal_anomaly.reshape(rows, LANES)),
            in_hbm(humidity_amount.reshape(rows, LANES)),
            in_hbm(slab_condensate_amount.reshape(rows, LANES)),
            *opacities,
            *scene,
        )
    words = exchange(words, "slab", FIRST_SLAB)
    with jax.named_scope("radiate"):
        radiance = pl.pallas_call(
            radiate_kernel,
            out_shape=pltpu.VMEM((DISKS, HALF, LANES), jnp.bfloat16),
            in_specs=[WHOLE] * 6 + [ANY] * 4,
            out_specs=WHOLE,
            scratch_shapes=prepared
            + [level_cols, level_cols, pltpu.VMEM((LEVELS + 8, LANES), f32), level_cols]
            + spread_room,
            compiler_params=SMALL,
        )(in_vmem(words), *ready, *opacities)
    radiance = exchange(radiance, "disk", FIRST_DISK)
    with jax.named_scope("pixels"):
        pixels = pl.pallas_call(
            pixel_kernel,
            out_shape=jax.ShapeDtypeStruct((HOURS * BANDS, PIX), f32),
            in_specs=[WHOLE] * 2 + [ANY] * 2,
            scratch_shapes=[mixed] + blend_room,
            compiler_params=SMALL,
        )(in_vmem(radiance), mix, *scene)
    return pixels.reshape(HOURS, BANDS, PIX)


def solution(mesh):
    in_specs = (
        P(None, "slab", "disk"),
        P(None, "slab", "disk"),
        P(None, "slab", "disk"),
        P(None, "disk"),
        P(),
        P(),
        P(),
        P(None, ("slab", "disk")),
        P(None, ("slab", "disk")),
    )
    out_specs = P(None, None, ("slab", "disk"))
    return jax.shard_map(local, mesh=mesh, in_specs=in_specs, out_specs=out_specs, check_vma=False)
```

```python
import jax
import jax.numpy as jnp
from jax import lax
from jax.experimental import pallas as pl
from jax.experimental.pallas import tpu as pltpu
from jax.sharding import PartitionSpec as P

HOURS = 2
BANDS = 16
GPB = 7
LEVELS = 128
TAPS = 4
COLS = 32
DISKS = 4
SECTOR = 4096
PIX = 512
HALF = BANDS // 2
LANES = 128
FIRST_SLAB = 75
FIRST_DISK = 2
EARLY = 3
STEP = 32
LOG2E = 1.4426950408889634

HUM_LOW, HUM_STEP = 0.2, 1.8 / 65535.0
CON_LOW, CON_STEP = 0.1, 1.9 / 65535.0
T4_SCALE = float(2**28)


def code16(x, low, step):
    q = ((x - low) * (1.0 / step) + 0.5).astype(jnp.int32)
    return jnp.clip(q, 0, 65535)


def swapped_group(size, first):
    if size == DISKS:
        return [2, 0, 3, 1]
    return [first if i == 0 else 0 if i == first else i for i in range(size)]


def swap_rows(ref):
    if FIRST_SLAB:
        held = ref[0:1, :]
        ref[0:1, :] = ref[FIRST_SLAB : FIRST_SLAB + 1, :]
        ref[FIRST_SLAB : FIRST_SLAB + 1, :] = held


def turn(x, shift):
    return x if isinstance(shift, int) and shift == 0 else pltpu.roll(x, shift, 1)


def is_early():
    return lax.rem(lax.axis_index("slab") // 2, 8) < EARLY


def fetch(pairs, sem_ref):
    copies = [pltpu.make_async_copy(src, dst, sem_ref.at[k]) for k, (src, dst) in enumerate(pairs)]
    for copy in copies:
        copy.start()
    return copies


def pack(temp_ref, hum_ref, con_ref, copies, out_ref):
    rows = SECTOR // LANES
    lane = lax.broadcasted_iota(jnp.int32, (rows, LANES), 1) // COLS
    copies[0].wait()
    t2 = temp_ref[...] * temp_ref[...]
    t4 = (t2 * t2 * T4_SCALE).astype(jnp.int32)
    copies[1].wait()
    hum = code16(hum_ref[...], HUM_LOW, HUM_STEP)
    copies[2].wait()
    con = code16(con_ref[...], CON_LOW, CON_STEP)
    gas = (hum << 16) | con
    parts = (gas[:rows], gas[rows:], t4[:rows], t4[rows:])
    for dest in range(LANES // COLS):
        word = None
        for spot, part in enumerate(parts):
            moved = turn(part, (spot - dest) % 4 * COLS)
            word = moved if word is None else jnp.where(lane == spot, moved, word)
        out_ref[pl.ds(dest, rows, stride=LANES // COLS), :] = word
    swap_rows(out_ref)


def spread(mol_hbm, con_hbm, planck_hbm, over_hbm, gas_ref, cloud_ref, start_ref, weight_ref, overcast_ref, room):
    mol_ref, con_ref, planck_ref, over_ref, sem_ref = room
    strip = lax.axis_index("slab")
    group = LANES // COLS
    block = over_hbm.at[:, pl.ds(pl.multiple_of(strip // group * LANES, LANES), LANES)]
    for copy in fetch(
        ((mol_hbm, mol_ref), (con_hbm, con_ref), (planck_hbm, planck_ref), (block, over_ref)), sem_ref
    ):
        copy.wait()
    lane = lax.broadcasted_iota(jnp.int32, (HALF, LANES), 1)
    first = lane < LANES // 2
    con = jnp.broadcast_to(con_ref[...], (HALF, con_ref.shape[1]))
    planck = jnp.broadcast_to(planck_ref[...], (HALF, planck_ref.shape[1]))
    glane = lax.broadcasted_iota(jnp.int32, con.shape, 1)
    grow = lax.broadcasted_iota(jnp.int32, con.shape, 0)

    def column(values, j):
        low = jnp.sum(jnp.where(glane == grow * GPB + j, values, 0.0), axis=1, keepdims=True)
        high = jnp.sum(
            jnp.where(glane == (grow + HALF) * GPB + j, values, 0.0), axis=1, keepdims=True
        )
        return jnp.where(
            first, jnp.broadcast_to(low, (HALF, LANES)), jnp.broadcast_to(high, (HALF, LANES))
        )

    for j in range(GPB):
        cloud_ref[j] = column(con, j) * -LOG2E
        weight = column(planck, j)
        start_ref[j] = jnp.log(weight) * LOG2E
        total = weight if j == 0 else total + weight
    weight_ref[...] = total

    overcast = None
    for spot in range(group):
        row = jnp.broadcast_to(over_ref[spot % HOURS : spot % HOURS + 1, :], (HALF, LANES))
        row = pltpu.roll(row, (spot - strip % group + group) % group * COLS, 1)
        overcast = row if overcast is None else jnp.where(lane // COLS == spot, row, overcast)
    overcast_ref[...] = overcast.astype(jnp.float32)

    span = LANES // 4
    shape = (span * HALF, LANES)
    pick = lax.broadcasted_iota(jnp.int32, shape, 1) % span == (
        lax.broadcasted_iota(jnp.int32, shape, 0) // HALF
    )
    half_of = lambda axis: lax.broadcasted_iota(jnp.int32, (LANES, LANES), axis) // (LANES // 2)
    same_half = (half_of(0) == half_of(1)).astype(jnp.float32).astype(jnp.bfloat16)

    def levels(q, _):
        for j in range(GPB):
            row = None
            for half in range(2):
                tile = mol_ref[pl.ds(half * HALF * GPB + j, HALF, stride=GPB), :] * -LOG2E
                high = tile.astype(jnp.bfloat16).astype(jnp.float32)
                for k, piece in enumerate((high, tile - high)):
                    spot = 2 * half + k
                    moved = turn(piece, (spot - q + 4) % 4 * span)
                    row = moved if row is None else jnp.where(lane // span == spot, moved, row)
            rows = jnp.broadcast_to(row[None], (span, HALF, LANES)).reshape(shape)
            rows = jnp.where(pick, rows, 0.0).astype(jnp.bfloat16)
            wide = jnp.dot(rows, same_half, preferred_element_type=jnp.float32)
            start = pl.multiple_of(q * span, span)
            gas_ref[pl.ds(start, span), j] = wide.reshape(span, HALF, LANES)
        return 0

    lax.fori_loop(0, 4, levels, 0)


def blend(source_hbm, factor_hbm, mix_ref, room):
    source_ref, factor_ref, sem_ref = room
    for copy in fetch(((source_hbm, source_ref), (factor_hbm, factor_ref)), sem_ref):
        copy.wait()
    strip_cols = DISKS * COLS
    col = lax.broadcasted_iota(jnp.int32, (strip_cols, PIX), 0)
    source = source_ref[...]
    local = source // SECTOR * COLS + source % COLS
    mix = jnp.zeros((strip_cols, PIX), jnp.float32)
    for tap in range(TAPS):
        mix = mix + jnp.where(col == local[tap : tap + 1], factor_ref[tap : tap + 1, :], 0.0)
    high = mix.astype(jnp.bfloat16)
    mix_ref[pl.ds(0, strip_cols), :] = high
    mix_ref[pl.ds(strip_cols, strip_cols), :] = (mix - high.astype(jnp.float32)).astype(jnp.bfloat16)


def pack_kernel(
    temp_hbm, hum_hbm, con_hbm, mol_hbm, cond_hbm, planck_hbm, over_hbm, source_hbm, factor_hbm,
    word_ref, gas_ref, cloud_ref, start_ref, weight_ref, overcast_ref, mix_ref,
    temp_ref, hum_ref, con_ref, field_sem, *room,
):
    fields = (temp_hbm, temp_ref), (hum_hbm, hum_ref), (con_hbm, con_ref)
    pack(temp_ref, hum_ref, con_ref, fetch(fields, field_sem), word_ref)

    @pl.when(is_early())
    def _():
        spread(
            mol_hbm, cond_hbm, planck_hbm, over_hbm,
            gas_ref, cloud_ref, start_ref, weight_ref, overcast_ref, room[:5],
        )
        blend(source_hbm, factor_hbm, mix_ref, room[5:])


def radiate(word_ref, gas_ref, cloud_ref, start_ref, weight_ref, overcast_ref, out_ref, rows):
    hum_ref, con_ref, t4_ref, diff_ref = rows
    word = word_ref[...]
    swapped = pltpu.roll(word, LANES // 2, 1)
    first = lax.broadcasted_iota(jnp.int32, word.shape, 1) < LANES // 2
    gas = jnp.where(first, word, swapped)
    t4 = jnp.where(first, swapped, word)
    hum = lax.shift_right_logical(gas, 16)
    con = gas & 65535
    hum_ref[...] = hum.astype(jnp.float32) * HUM_STEP + HUM_LOW
    con_ref[...] = (con.astype(jnp.float32) * CON_STEP + CON_LOW) * overcast_ref[0:1, :]
    t4_ref[pl.ds(0, LEVELS), :] = t4.astype(jnp.float32) * (1.0 / T4_SCALE)
    for by_sender in (hum_ref, con_ref, t4_ref):
        swap_rows(by_sender)
    t4_ref[pl.ds(LEVELS, 1), :] = t4_ref[pl.ds(LEVELS - 1, 1), :]
    diff_ref[...] = t4_ref[pl.ds(1, LEVELS), :] - t4_ref[pl.ds(0, LEVELS), :]

    clouds = [cloud_ref[j] for j in range(GPB)]

    def step(i, carry):
        depth, total = list(carry[0]), carry[1]
        for k in range(STEP):
            level = STEP * i + k
            hum_row = hum_ref[pl.ds(level, HALF, stride=0), :]
            con_row = con_ref[pl.ds(level, HALF, stride=0), :]
            diff_row = diff_ref[pl.ds(level, HALF, stride=0), :]
            for j in range(GPB):
                depth[j] = depth[j] + (gas_ref[level, j] * hum_row + clouds[j] * con_row)
            seen = [jnp.exp2(x) for x in depth]
            while len(seen) > 1:
                seen = [a + b for a, b in zip(seen[::2], seen[1::2])] + seen[len(seen) // 2 * 2 :]
            total = total + diff_row * seen[0]
        return tuple(depth), total

    starts = tuple(start_ref[j] for j in range(GPB))
    _, total = lax.fori_loop(0, LEVELS // STEP, step, (starts, jnp.zeros((HALF, LANES), jnp.float32)))
    top = t4_ref[pl.ds(0, HALF, stride=0), :]
    band = ((weight_ref[...] * top + total) / GPB).astype(jnp.bfloat16)
    for owner in range(DISKS):
        out_ref[owner] = band


def radiate_kernel(
    word_ref, gas_ref, cloud_ref, start_ref, weight_ref, overcast_ref, mol_hbm, cond_hbm, planck_hbm, over_hbm,
    out_ref,
    own_gas, own_cloud, own_start, own_weight, own_overcast, hum_ref, con_ref, t4_ref, diff_ref, *room,
):
    rows = hum_ref, con_ref, t4_ref, diff_ref

    @pl.when(is_early())
    def _():
        radiate(word_ref, gas_ref, cloud_ref, start_ref, weight_ref, overcast_ref, out_ref, rows)

    @pl.when(jnp.logical_not(is_early()))
    def _():
        own = own_gas, own_cloud, own_start, own_weight, own_overcast
        spread(mol_hbm, cond_hbm, planck_hbm, over_hbm, *own, room)
        radiate(word_ref, *own, out_ref, rows)


def pixel_kernel(rad_ref, mix_ref, source_hbm, factor_hbm, out_ref, own_mix, *room):
    lane = lax.broadcasted_iota(jnp.int32, (HALF, LANES), 1) // COLS
    sender = swapped_group(DISKS, FIRST_DISK)
    rows = []
    for hour in range(HOURS):
        for half in range(2):
            spot = half * HOURS + hour
            row = None
            for disk in range(DISKS):
                moved = turn(rad_ref[sender.index(disk)].astype(jnp.float32), (disk - spot) % 4 * COLS)
                row = moved if row is None else jnp.where(lane == disk, moved, row)
            rows.append(row)
    rad = jnp.concatenate(rows, axis=0).astype(jnp.bfloat16)
    rad = jnp.concatenate([rad, rad], axis=1)

    @pl.when(is_early())
    def _():
        out_ref[...] = jnp.dot(rad, mix_ref[...], preferred_element_type=jnp.float32)

    @pl.when(jnp.logical_not(is_early()))
    def _():
        blend(source_hbm, factor_hbm, own_mix, room)
        out_ref[...] = jnp.dot(rad, own_mix[...], preferred_element_type=jnp.float32)


ANY = pl.BlockSpec(memory_space=pl.ANY)
WHOLE = pl.BlockSpec(memory_space=pltpu.VMEM)
SMALL = pltpu.CompilerParams(vmem_limit_bytes=16 << 20)


def in_vmem(x):
    return pltpu.with_memory_space_constraint(x, pltpu.VMEM)


def in_hbm(x):
    return pltpu.with_memory_space_constraint(x, pltpu.HBM)


def exchange(x, axis, first):
    group = swapped_group(lax.axis_size(axis), first)
    return lax.all_to_all(x, axis, 0, 0, axis_index_groups=[group], tiled=True)


def local(
    thermal_anomaly,
    humidity_amount,
    slab_condensate_amount,
    overcast_indicator,
    molecular_opacity,
    condensate_opacity,
    planck_quadrature_factor,
    scene_contributing_profiles,
    scene_interpolation_factors,
):
    f32 = jnp.float32
    rows = HOURS * SECTOR // LANES
    field = pltpu.VMEM((rows, LANES), f32)
    level_cols = pltpu.VMEM((LEVELS, LANES), f32)
    per_point = pltpu.VMEM((GPB, HALF, LANES), f32)
    prepared = [
        pltpu.VMEM((LEVELS, GPB, HALF, LANES), f32),
        per_point,
        per_point,
        pltpu.VMEM((HALF, LANES), f32),
        pltpu.VMEM((HALF, LANES), f32),
    ]
    mixed = pltpu.VMEM((2 * DISKS * COLS, PIX), jnp.bfloat16)
    points = condensate_opacity.shape[0]
    spread_room = [
        pltpu.VMEM((points, LEVELS), f32),
        pltpu.VMEM((1, points), f32),
        pltpu.VMEM((1, points), f32),
        pltpu.VMEM((HOURS, LANES), jnp.int32),
        pltpu.SemaphoreType.DMA((4,)),
    ]
    blend_room = [
        pltpu.VMEM((TAPS, PIX), jnp.int32),
        pltpu.VMEM((TAPS, PIX), f32),
        pltpu.SemaphoreType.DMA((2,)),
    ]
    opacities = [
        in_hbm(molecular_opacity),
        in_hbm(condensate_opacity.reshape(1, -1)),
        in_hbm(planck_quadrature_factor.reshape(1, -1)),
        in_hbm(overcast_indicator),
    ]
    scene = [in_hbm(scene_contributing_profiles), in_hbm(scene_interpolation_factors)]
    with jax.named_scope("pack"):
        words, *ready, mix = pl.pallas_call(
            pack_kernel,
            out_shape=(pltpu.VMEM((LEVELS, LANES), jnp.int32), *prepared, mixed),
            in_specs=[ANY] * 9,
            out_specs=[WHOLE] * 7,
            scratch_shapes=[field] * 3 + [pltpu.SemaphoreType.DMA((3,))] + spread_room + blend_room,
            compiler_params=SMALL,
        )(
            in_hbm(thermal_anomaly.reshape(rows, LANES)),
            in_hbm(humidity_amount.reshape(rows, LANES)),
            in_hbm(slab_condensate_amount.reshape(rows, LANES)),
            *opacities,
            *scene,
        )
    words = exchange(words, "slab", FIRST_SLAB)
    with jax.named_scope("radiate"):
        radiance = pl.pallas_call(
            radiate_kernel,
            out_shape=pltpu.VMEM((DISKS, HALF, LANES), jnp.bfloat16),
            in_specs=[WHOLE] * 6 + [ANY] * 4,
            out_specs=WHOLE,
            scratch_shapes=prepared
            + [level_cols, level_cols, pltpu.VMEM((LEVELS + 8, LANES), f32), level_cols]
            + spread_room,
            compiler_params=SMALL,
        )(in_vmem(words), *ready, *opacities)
    radiance = exchange(radiance, "disk", FIRST_DISK)
    with jax.named_scope("pixels"):
        pixels = pl.pallas_call(
            pixel_kernel,
            out_shape=jax.ShapeDtypeStruct((HOURS * BANDS, PIX), f32),
            in_specs=[WHOLE] * 2 + [ANY] * 2,
            scratch_shapes=[mixed] + blend_room,
            compiler_params=SMALL,
        )(in_vmem(radiance), mix, *scene)
    return pixels.reshape(HOURS, BANDS, PIX)


def solution(mesh):
    in_specs = (
        P(None, "slab", "disk"),
        P(None, "slab", "disk"),
        P(None, "slab", "disk"),
        P(None, "disk"),
        P(),
        P(),
        P(),
        P(None, ("slab", "disk")),
        P(None, ("slab", "disk")),
    )
    out_specs = P(None, None, ("slab", "disk"))
    return jax.shard_map(local, mesh=mesh, in_specs=in_specs, out_specs=out_specs, check_vma=False)
```
